256 devices in a mesh: segment: 2 (over core), expert: 128 (over x, z, y).
Axes of the slice: x: 4, y: 4, z: 8, core: 2. Of those that a mesh axis runs over, the one named last changes fastest.
Arguments:
- latents: float32 [4, 4096, 16], P(None, 'expert'), may hold values from -6 to 6
- cond: float32 [8, 1536], replicated, may hold values from -3 to 3
- w_embed: float32 [16, 1536], replicated, may hold values from -1.5 to 1.5
- modulation: float32 [2, 8, 3, 1536], P('segment'), may hold values from -4.5 to 4.5
- router: bfloat16 [2, 1536, 16], P('segment'), may hold values from -0.15625 to 0.15625
- w_in: bfloat16 [2, 128, 1536, 768], P('segment', 'expert'), may hold values from -0.15625 to 0.15625
- w_out: bfloat16 [2, 128, 768, 1536], P('segment', 'expert'), may hold values from -0.078125 to 0.078125
- routes: int32 [2, 4, 4096, 2], P('segment', None, 'expert'), may hold values from 0 to 15, all different within a row; in each aligned block of 32 rows (0 to 31, 32 to 63, ..., all dimensions but the last counted through in order) at most 5 rows name the same one
- w_final: bfloat16 [1536, 16], replicated, may hold values from -0.15625 to 0.15625
Outputs:
- x_next: float32 [4, 4096, 16], P('segment', 'expert')
- post_mean: float32 [8, 256, 16], replicated
- post_var: float32 [8, 256, 16], replicated
The draws below stay inside these ranges and needn't reach their ends.
Inputs may be any that keep to these rules, and one draw needn't show every extreme that they name: `routes`: in every layer and micro-batch, no expert is named by more than 5 of one device's 32 rows, a bound that some block reaches of them; a row names two different experts.
All inputs are finite; a program needn't handle non-finite values.
Results may differ from the reference program's by a relative error of at most 0.01.
Values may be sent and summed in bfloat16 or wider, within the bound.
A program may use at most 128 MiB of HBM per device.

```python
import math
import jax
import jax.numpy as jnp
import numpy as np
from jax import lax

D = 1536
HIDDEN_SIZE = 6144
EXPERTS = 16
PATCH = 16
SAMPLES = 8
SEQ = 256
MICRO = 4
ROWS_DEV = 32
CAP = 5
SPLITS = 8
LAYERS = 2
ROWS = 4096
PROMPTS = 8
N_EXPERT = 128


def shard_levels(own_key, dims, shards, least, high):
    gain = 1.0
    for dim, parts in shards:
        draws = jax.random.uniform(jax.random.fold_in(jax.random.fold_in(own_key, 6), dim), (parts,), jnp.float32, least / len(shards), high / len(shards))
        gain = gain * jnp.repeat(jnp.exp(draws), dims[dim] // parts).reshape((-1,) + (1,) * (len(dims) - 1 - dim))
    return gain


def deal_out(stream_key, own, number, rows, amount, top, bound, lean):
    sequence = jax.random.permutation(stream_key, amount)
    packed, usual = shares(amount, rows * top, bound, lean, True), shares(amount, rows * top, bound, lean, False)
    places = jnp.arange(amount)

    def named(lengths, rotation):
        used = int((lengths > 0).sum())
        fixed = max(1, used // 4)
        moved = fixed + (places - fixed + rotation * (used - fixed)) % max(1, amount - fixed)
        return jnp.zeros((amount,), jnp.int32).at[sequence[jnp.where(places < fixed, places, moved)]].set(jnp.asarray(lengths, jnp.int32))

    lengths = jnp.where(number % 4 == 0, named(packed, number // 4), named(usual, number - number // 4 - 1))
    mixed = jax.random.permutation(jax.random.fold_in(own, 3), amount)
    donor, sink = mixed[0:amount // 2 * 2:2], mixed[1:amount // 2 * 2:2]
    slack = jnp.minimum(lengths[donor] - 1, bound - lengths[sink]) // 2
    slack = jnp.where((donor == sequence[0]) | (sink == sequence[0]) | (lengths[sink] == 0), 0, jnp.maximum(slack, 0))
    moved = jax.random.randint(jax.random.fold_in(own, 4), (amount // 2,), 0, 1 << 20) % (slack + 1)
    lengths = lengths.at[donor].add(-moved).at[sink].add(moved)
    items = jnp.searchsorted(jnp.cumsum(lengths), jnp.arange(rows * top), side="right").astype(jnp.int32)
    grid = items.reshape(top, rows).T
    grid = grid[jax.random.permutation(jax.random.fold_in(own, 1), rows)]
    rotation = jax.random.randint(jax.random.fold_in(own, 2), (rows, 1), 0, top)
    return jnp.take_along_axis(grid, (jnp.arange(top)[None, :] + rotation) % top, axis=1)


def shares(number_of, total, most, slope, full):
    weights = [(1 << 20) // math.isqrt(standing ** slope) + 1 for standing in range(1, number_of + 1)]
    largest = most if full else min(most, max(-(-total // number_of), total * weights[0] // sum(weights)))
    least = 1 if total - largest >= number_of - 1 else 0
    counts, rest = [largest] + [least] * (number_of - 1), total - largest - least * (number_of - 1)
    while rest > 0:
        free = [i for i in range(1, number_of) if counts[i] < largest] or [i for i in range(1, number_of) if counts[i] < most]
        pool, remaining = sum([weights[i] for i in free]), rest
        for i in free:
            more = min(most - counts[i], max(1, remaining * weights[i] // pool), rest)
            counts[i] = counts[i] + more
            rest = rest - more
    return np.array(counts)


def noise(own_key, shape, deviation, limit, cuts=(), kind=jnp.bfloat16):
    values = deviation * jax.random.normal(own_key, shape, jnp.float32)
    if cuts:
        values = values * shard_levels(own_key, shape, cuts, -0.22, 0.18)
    return jnp.clip(values, -limit, limit).astype(kind)


def setup_inputs(seed: int = 0) -> dict:
    seeds = jax.random.split(jax.random.key(seed), 10)
    latents = noise(seeds[0], (MICRO, ROWS, PATCH), 1.0, 6.0, ((1, 128),), jnp.float32)
    cond = noise(seeds[1], (PROMPTS, D), 0.5, 3.0, (), jnp.float32)
    w_embed = noise(seeds[2], (PATCH, D), PATCH ** -0.5, 1.5, (), jnp.float32)
    modulation = noise(seeds[3], (LAYERS, PROMPTS, 3, D), 1.5, 4.5, ((0, 2),), jnp.float32)
    router = noise(seeds[4], (LAYERS, D, EXPERTS), D ** -0.5, 0.15625, ((0, 2),))
    w_in = noise(seeds[5], (LAYERS, EXPERTS * SPLITS, D, HIDDEN_SIZE // SPLITS), D ** -0.5, 0.15625, ((0, 2), (1, 128)))
    w_out = noise(seeds[6], (LAYERS, EXPERTS * SPLITS, HIDDEN_SIZE // SPLITS, D), HIDDEN_SIZE ** -0.5, 0.078125, ((0, 2), (1, 128)))
    routes_keys = jax.random.split(jax.random.fold_in(seeds[7], 1), LAYERS * MICRO * ROWS // ROWS_DEV)
    routes_turns = jax.random.permutation(jax.random.fold_in(seeds[7], 3), LAYERS * MICRO * ROWS // ROWS_DEV)
    routes = jax.vmap(lambda own, number: deal_out(jax.random.fold_in(seeds[7], 2), own, number, ROWS_DEV, EXPERTS, 2, CAP, 2))(routes_keys, routes_turns).reshape((LAYERS, MICRO, ROWS, 2))
    w_final = noise(seeds[8], (D, PATCH), D ** -0.5, 0.15625)
    return dict(latents=latents, cond=cond, w_embed=w_embed, modulation=modulation, router=router, w_in=w_in, w_out=w_out, routes=routes, w_final=w_final)


epsilon = 1e-06
time_step = 0.25
time_left = 0.5

def normalize(values_in):
    values_in = values_in.astype(jnp.float32)
    centered = values_in - lax.optimization_barrier(jnp.mean(values_in, axis=-1, keepdims=True))
    variance = lax.optimization_barrier(jnp.mean(centered * centered, axis=-1, keepdims=True))
    return centered * lax.rsqrt(variance + epsilon)

def position_table(positions, model_width):
    half_width = model_width // 2
    frequency = jnp.exp(-jnp.log(10000.0) * jnp.arange(half_width, dtype=jnp.float32) / half_width)
    angles = positions.astype(jnp.float32)[:, None] * frequency[None, :]
    return jnp.concatenate([jnp.sin(angles), jnp.cos(angles)], axis=-1)

def moe_layer(hidden, mod_rows, gate_table, first_all, second_all, chosen):
    row_count = hidden.shape[0]
    splits = N_EXPERT // EXPERTS
    inner_width = first_all.shape[2]
    normed = (normalize(hidden) * (1.0 + mod_rows[:, 1]) + mod_rows[:, 0]).astype(jnp.bfloat16)
    logits = jnp.dot(normed, gate_table, preferred_element_type=jnp.float32)
    picked = jnp.take_along_axis(logits, chosen, axis=1)
    gate_probs = jax.nn.sigmoid(picked)
    mix_weights = gate_probs / lax.optimization_barrier(jnp.sum(gate_probs, axis=1, keepdims=True))
    flat_hot = (chosen.reshape(N_EXPERT, ROWS_DEV * 2)[:, :, None] == jnp.arange(EXPERTS, dtype=jnp.int32)[None, None, :]).astype(jnp.int32)
    before = jnp.cumsum(flat_hot, axis=1) - flat_hot
    slot_index = lax.optimization_barrier(jnp.sum(flat_hot * before, axis=2))
    placement = (jnp.arange(N_EXPERT, dtype=jnp.int32)[:, None] * CAP + slot_index).reshape(-1).astype(jnp.int32)
    target = chosen.reshape(-1).astype(jnp.int32)
    repeated = jnp.repeat(normed, 2, axis=0)
    buffers = jnp.zeros((EXPERTS, N_EXPERT * CAP, D), jnp.bfloat16).at[target, placement].set(repeated)

    def expert(operand):
        buffer, w_first, w_second = operand
        inner_act = jnp.einsum('nd,sdh->snh', buffer.astype(jnp.float32), w_first.astype(jnp.float32))
        inner_act = jax.nn.gelu(inner_act, approximate=True).astype(jnp.bfloat16)
        partial_value = jnp.einsum('snh,shd->snd', inner_act.astype(jnp.float32), w_second.astype(jnp.float32)).astype(jnp.bfloat16)
        return lax.optimization_barrier(jnp.sum(partial_value.astype(jnp.float32), axis=0))
    results = lax.map(expert, (buffers, first_all.reshape(EXPERTS, splits, D, inner_width), second_all.reshape(EXPERTS, splits, inner_width, D)))
    gathered = results[target, placement].reshape(row_count, 2, D)
    moe_out = lax.optimization_barrier(jnp.sum(mix_weights[:, :, None] * gathered, axis=1))
    return (hidden.astype(jnp.float32) + mod_rows[:, 2] * moe_out).astype(jnp.bfloat16)

def reference(latents, cond, w_embed, modulation, router, w_in, w_out, routes, w_final):
    row_count = ROWS_DEV * N_EXPERT
    next_list = []
    clean_list = []
    for micro in range(MICRO):
        global_rows = micro * row_count + jnp.arange(row_count, dtype=jnp.int32)
        prompt = (global_rows // (SEQ * SAMPLES)).astype(jnp.int32)
        positions = global_rows % SEQ
        latent_rows = latents[micro]
        hidden = jnp.dot(latent_rows, w_embed, precision=lax.Precision.HIGHEST) + position_table(positions, D) + cond[prompt]
        hidden = hidden.astype(jnp.bfloat16)
        for layer_index in range(LAYERS):
            hidden = moe_layer(hidden, modulation[layer_index][prompt], router[layer_index], w_in[layer_index], w_out[layer_index], routes[layer_index, micro])
        final_norm = normalize(hidden).astype(jnp.bfloat16)
        velocity = jnp.dot(final_norm, w_final, preferred_element_type=jnp.float32)
        next_list.append(latent_rows + time_step * velocity)
        clean_list.append(latent_rows + time_left * velocity)
    x_next = jnp.stack(next_list)
    clean = jnp.stack(clean_list).reshape(PROMPTS, SAMPLES, SEQ, PATCH)
    map_total = lax.optimization_barrier(jnp.sum(clean, axis=1))
    square_sum = lax.optimization_barrier(jnp.sum(clean * clean, axis=1))
    mean_map = map_total / SAMPLES
    variance = square_sum / SAMPLES - mean_map * mean_map
    return (x_next, mean_map, variance)
```

```python
import functools

import jax
import jax.numpy as jnp
from jax import lax
from jax.experimental import pallas as pl
from jax.experimental.pallas import tpu as pltpu
from jax.sharding import PartitionSpec as P

SAMPLES = 8
SEQ = 256
CAP = 5
PAD = 8

epsilon = 1e-06
time_step = 0.25
time_left = 0.5

f32 = jnp.float32
bf16 = jnp.bfloat16
MESH = pl.DeviceIdType.MESH


def normalize(values_in):
    centered = values_in - jnp.mean(values_in, axis=-1, keepdims=True)
    variance = jnp.mean(centered * centered, axis=-1, keepdims=True)
    return centered * lax.rsqrt(variance + epsilon)


def dot(left, right):
    return jnp.dot(left, right, preferred_element_type=f32)


def position_table(positions, model_width):
    half_width = model_width // 2
    frequency = jnp.exp(-jnp.log(10000.0) * jnp.arange(half_width, dtype=f32) / half_width)
    angles = positions.astype(f32)[:, None] * frequency[None, :]
    return jnp.concatenate([jnp.sin(angles), jnp.cos(angles)], axis=-1)


def kernel(
    sizes,
    hidden_in, latents_in, w_final, choice_in, spread_in, modulation, router_in, w_first, w_second,
    next_out, mean_out, var_out,
    hid, mix, choice, spread, mods, router, first, second,
    out_send, out_recv, rows_in, rows_out, parts, home_send, home_recv,
    stats, stats_recv, maps, send_sems, recv_sems, load_sems, push_sems, land_sems,
):
    groups, members, samples, rows, width, flat = sizes
    half = members // 2
    group_rows = groups * CAP
    core = lax.axis_index("segment")
    device = lax.axis_index("expert")
    group, member = device // members, device % members
    prompt_half, sample = group // samples, group % samples
    halves = groups // samples
    other = 1 - core

    def expert_at(to_group, to_member):
        return {"expert": to_group * members + to_member}

    def load_pairs(micro_core):
        pairs = [
            (choice_in.at[pl.ds(2 * micro_core, 2)], choice.at[core]),
            (spread_in.at[pl.ds(2 * micro_core, 2)], spread.at[core]),
            (router_in, router.at[core]),
        ]
        for member_micro in range(2):
            prompt = (2 * micro_core + member_micro) * halves + prompt_half
            pairs.append((modulation.at[0, prompt], mods.at[core, member_micro]))
        pairs.append((w_first.at[0, 0], first.at[core]))
        pairs.append((w_second.at[0, 0], second.at[core]))
        return pairs

    own_loads = [
        pltpu.make_async_copy(src, dst, load_sems.at[i]) for i, (src, dst) in enumerate(load_pairs(core))
    ]
    pushes = [
        pltpu.make_async_remote_copy(
            src_ref=src, dst_ref=dst, send_sem=push_sems.at[i], recv_sem=land_sems.at[i],
            device_id={"segment": other}, device_id_type=MESH,
        )
        for i, (src, dst) in enumerate(load_pairs(other))
    ]
    for copy in own_loads[:5]:
        copy.start()
    for copy in pushes:
        copy.start()
    for copy in own_loads[5:]:
        copy.start()

    slots = groups * PAD
    row_id = lax.broadcasted_iota(jnp.int32, (group_rows, slots), 0)
    slot_id = lax.broadcasted_iota(jnp.int32, (group_rows, slots), 1)
    within = slot_id & (PAD - 1)
    packing = jnp.where((row_id == CAP * (slot_id >> 3) + within) & (within < CAP), 1.0, 0.0).astype(bf16)
    row_id_t = lax.broadcasted_iota(jnp.int32, (slots, group_rows), 1)
    slot_id_t = lax.broadcasted_iota(jnp.int32, (slots, group_rows), 0)
    within_t = slot_id_t & (PAD - 1)
    unpacking = jnp.where(
        (row_id_t == CAP * (slot_id_t >> 3) + within_t) & (within_t < CAP), 1.0, 0.0
    ).astype(bf16)

    def wait_bytes(ref, sem):
        pltpu.make_async_copy(ref, ref, sem).wait()

    def send_across(unit, source, target, stage):
        target[unit, group] = source[unit, group]

        @pl.loop(1, groups)
        def _(k):
            to_group = (group + k) % groups
            pltpu.make_async_remote_copy(
                src_ref=source.at[unit, to_group], dst_ref=target.at[unit, group],
                send_sem=send_sems.at[stage, unit], recv_sem=recv_sems.at[stage, unit],
                device_id=expert_at(to_group, member), device_id_type=MESH,
            ).start()

    def front(layer, micro):
        unit = 2 * layer + micro
        shift, scale = mods[layer, micro, 0:1], mods[layer, micro, 1:2]
        normed = (normalize(hid[micro].astype(f32)) * (1.0 + scale) + shift).astype(bf16)
        logits = dot(normed, router[layer])
        hot_0, hot_1 = choice[layer, micro, 0].astype(f32), choice[layer, micro, 1].astype(f32)
        prob_0 = lax.logistic(jnp.sum(hot_0 * logits, axis=1, keepdims=True))
        prob_1 = lax.logistic(jnp.sum(hot_1 * logits, axis=1, keepdims=True))
        weights = (hot_0 * prob_0 + hot_1 * prob_1) / (prob_0 + prob_1)
        mix[micro] = weights
        packed = dot(spread[layer, micro], normed)
        out_send[unit] = packed.reshape(groups, PAD, width).astype(bf16)
        send_across(unit, out_send, out_recv, 0)

    def gather(layer, micro):
        unit = 2 * layer + micro
        wait_bytes(out_recv.at[unit, pl.ds(0, groups - 1)], recv_sems.at[0, unit])
        arrived = out_recv[unit].astype(f32).reshape(slots, width).astype(bf16)
        rows_in[unit, member] = dot(packing, arrived).astype(bf16)

        @pl.loop(1, members)
        def _(k):
            to_member = (member + k) % members
            pltpu.make_async_remote_copy(
                src_ref=rows_in.at[unit, member], dst_ref=rows_in.at[unit, member],
                send_sem=send_sems.at[1, unit], recv_sem=recv_sems.at[1, unit],
                device_id=expert_at(group, to_member), device_id_type=MESH,
            ).start()

    def compute(layer, micro):
        unit = 2 * layer + micro
        wait_bytes(rows_in.at[unit, pl.ds(0, members - 1)], recv_sems.at[1, unit])

        @pl.loop(0, 2)
        def _(step):
            plane = (member // half + 1 + step) % 2
            block = pl.ds(plane * half, half)
            inner = dot(rows_in[unit, block].reshape(half * group_rows, width), first[layer])
            inner = jax.nn.gelu(inner, approximate=True).astype(bf16)
            partial = dot(inner, second[layer]).astype(bf16)
            rows_out[unit, block] = partial.reshape(half, group_rows, width)

            @pl.loop(0, half)
            def _(k):
                to_member = plane * half + (member + k) % half

                @pl.when(to_member != member)
                def _():
                    pltpu.make_async_remote_copy(
                        src_ref=rows_out.at[unit, to_member], dst_ref=parts.at[unit, member],
                        send_sem=send_sems.at[2, unit], recv_sem=recv_sems.at[2, unit],
                        device_id=expert_at(group, to_member), device_id_type=MESH,
                    ).start()

        parts[unit, member] = rows_out[unit, member]

    def send_home(layer, micro):
        unit = 2 * layer + micro
        wait_bytes(parts.at[unit, pl.ds(0, members - 1)], recv_sems.at[2, unit])
        total = parts[unit, 0].astype(f32)
        for k in range(1, members):
            total = total + parts[unit, k].astype(f32)
        spaced = dot(unpacking, total.astype(bf16))
        home_send[unit] = spaced.reshape(groups, PAD, width).astype(bf16)
        send_across(unit, home_send, home_recv, 3)

    def combine(layer, micro):
        unit = 2 * layer + micro
        wait_bytes(home_recv.at[unit, pl.ds(0, groups - 1)], recv_sems.at[3, unit])
        returned = home_recv[unit].astype(f32).reshape(slots, width).astype(bf16)
        weights = mix[micro]
        coarse = weights.astype(bf16)
        fine = (weights - coarse.astype(f32)).astype(bf16)
        moe = dot(coarse, returned) + dot(fine, returned)
        hid[micro] = (hid[micro].astype(f32) + mods[layer, micro, 2:3] * moe).astype(bf16)

    hid[...] = hidden_in[...]

    for copy in own_loads[:5]:
        copy.wait()
    for copy in pushes[:5]:
        copy.wait_recv()

    for micro in range(2):
        front(0, micro)

    @pl.loop(0, 2)
    def _(layer):
        @pl.loop(0, 2)
        def _(micro):
            gather(layer, micro)

        @pl.when(layer == 0)
        def _():
            for copy in own_loads[5:]:
                copy.wait()
            for copy in pushes[5:]:
                copy.wait_recv()

        @pl.loop(0, 2)
        def _(micro):
            compute(layer, micro)

        @pl.loop(0, 2)
        def _(micro):
            send_home(layer, micro)

        @pl.loop(0, 2)
        def _(micro):
            combine(layer, micro)

            @pl.when(layer == 0)
            def _():
                front(1, micro)

    lane = lax.broadcasted_iota(jnp.int32, (rows, 128), 1)
    row = lax.broadcasted_iota(jnp.int32, (rows, 128), 0)
    kept = (lane >> 4) == (row & 7)
    for micro in range(2):
        final = normalize(hid[micro].astype(f32)).astype(bf16)
        velocity = jnp.where(kept, dot(final, w_final[...]), 0.0)
        velocity = jnp.sum(velocity.reshape(flat, 8, 128), axis=1)
        start = latents_in[micro]
        next_out[micro] = start + time_step * velocity
        clean = start + time_left * velocity
        stats[pl.ds(2 * micro * flat, flat)] = clean
        stats[pl.ds((2 * micro + 1) * flat, flat)] = clean * clean

    stats_recv[sample] = stats[...]

    @pl.loop(1, samples)
    def _(k):
        to_sample = (sample + k) % samples
        pltpu.make_async_remote_copy(
            src_ref=stats, dst_ref=stats_recv.at[sample],
            send_sem=push_sems.at[7], recv_sem=land_sems.at[7],
            device_id=expert_at(prompt_half * samples + to_sample, member), device_id_type=MESH,
        ).start()

    wait_bytes(stats_recv.at[pl.ds(0, samples - 1)], land_sems.at[7])
    total = stats_recv[0]
    for k in range(1, samples):
        total = total + stats_recv[k]
    keys = 2 * halves * members
    key = (core * halves + prompt_half) * members + member
    maps[key] = total

    @pl.loop(1, keys)
    def _(k):
        to_key = (key + k) % keys
        to_core = to_key // (halves * members)
        to_half = (to_key // members) % halves
        pltpu.make_async_remote_copy(
            src_ref=maps.at[key], dst_ref=maps.at[key],
            send_sem=push_sems.at[8], recv_sem=land_sems.at[8],
            device_id={
                "segment": to_core, "expert": (to_half * samples + sample) * members + to_key % members
            },
            device_id_type=MESH,
        ).start()

    wait_bytes(maps.at[pl.ds(0, keys - 1)], land_sems.at[8])
    for from_key in range(keys):
        from_core, from_half, from_member = (
            from_key // (halves * members), (from_key // members) % halves, from_key % members
        )
        for micro in range(2):
            prompt = (2 * from_core + micro) * halves + from_half
            place = pl.ds(from_member * flat, flat)
            mean = maps[from_key, pl.ds(2 * micro * flat, flat)] / SAMPLES
            square = maps[from_key, pl.ds((2 * micro + 1) * flat, flat)] / SAMPLES
            mean_out[prompt, place] = mean
            var_out[prompt, place] = square - mean * mean

    for copy in pushes:
        copy.wait_send()
    wait_bytes(stats_recv.at[pl.ds(0, samples - 1)], push_sems.at[7])
    wait_bytes(maps.at[pl.ds(0, keys - 1)], push_sems.at[8])

    @pl.loop(0, 4)
    def _(unit):
        wait_bytes(out_recv.at[unit, pl.ds(0, groups - 1)], send_sems.at[0, unit])
        wait_bytes(rows_in.at[unit, pl.ds(0, members - 1)], send_sems.at[1, unit])
        wait_bytes(parts.at[unit, pl.ds(0, members - 1)], send_sems.at[2, unit])
        wait_bytes(home_recv.at[unit, pl.ds(0, groups - 1)], send_sems.at[3, unit])


def local(latents, cond, w_embed, modulation, router, w_in, w_out, routes, w_final):
    core = lax.axis_index("segment")
    device = lax.axis_index("expert")
    devices = lax.axis_size("expert")
    micro_count, rows, patch = latents.shape
    width, experts = router.shape[1], router.shape[2]
    hidden_slice = w_in.shape[3]
    members = devices // experts
    groups = experts
    rows_all = rows * devices
    flat = rows * patch // 128
    slots = groups * PAD
    group_rows = groups * CAP
    prompts = cond.shape[0]

    own = lax.dynamic_slice_in_dim(latents, 2 * core, 2, 0)
    row_start = (2 * core + jnp.arange(2)) * rows_all + device * rows
    prompt = row_start // (SEQ * SAMPLES)
    positions = (device * rows) % SEQ + jnp.arange(rows, dtype=jnp.int32)
    embedded = jnp.einsum("mrp,pd->mrd", own, w_embed, precision=lax.Precision.HIGHEST)
    cond_rows = jnp.stack([lax.dynamic_index_in_dim(cond, prompt[i], 0, keepdims=True) for i in range(2)])
    hidden = (embedded + position_table(positions, width) + cond_rows).astype(bf16)

    chosen = routes[0]
    hot = (chosen[..., None] == jnp.arange(experts, dtype=jnp.int32)).astype(bf16)
    earlier = jnp.tril(jnp.ones((rows, rows), bf16), -1)
    before = jnp.einsum("rs,mse->mre", earlier, hot[:, :, 0] + hot[:, :, 1], preferred_element_type=f32)
    slot = jnp.sum(before[:, :, None, :] * hot.astype(f32), axis=3).astype(jnp.int32)
    place = (chosen * PAD + slot).transpose(0, 2, 1)
    choice = (place[..., None] == jnp.arange(slots, dtype=jnp.int32)).astype(bf16)
    spread = (
        (place[:, 0, None, :] == jnp.arange(slots, dtype=jnp.int32)[:, None])
        | (place[:, 1, None, :] == jnp.arange(slots, dtype=jnp.int32)[:, None])
    ).astype(bf16)

    vmem = pl.BlockSpec(memory_space=pltpu.VMEM)
    left = pl.BlockSpec(memory_space=pl.ANY)
    keys = 2 * (groups // SAMPLES) * members
    sizes = (groups, members, SAMPLES, rows, width, flat)
    next_flat, mean_flat, var_flat = pl.pallas_call(
        functools.partial(kernel, sizes),
        out_shape=(
            jax.ShapeDtypeStruct((2, flat, 128), f32),
            jax.ShapeDtypeStruct((prompts, members * flat, 128), f32),
            jax.ShapeDtypeStruct((prompts, members * flat, 128), f32),
        ),
        in_specs=[vmem, vmem, vmem, vmem, vmem, left, vmem, left, left],
        out_specs=(vmem, vmem, vmem),
        scratch_shapes=[
            pltpu.VMEM((2, rows, width), bf16),
            pltpu.VMEM((2, rows, slots), f32),
            pltpu.VMEM((2, 2, 2, rows, slots), bf16),
            pltpu.VMEM((2, 2, slots, rows), bf16),
            pltpu.VMEM((2, 2, 3, width), f32),
            pltpu.VMEM((2, width, slots), bf16),
            pltpu.VMEM((2, width, hidden_slice), bf16),
            pltpu.VMEM((2, hidden_slice, width), bf16),
            pltpu.VMEM((4, groups, PAD, width), bf16),
            pltpu.VMEM((4, groups, PAD, width), bf16),
            pltpu.VMEM((4, members, group_rows, width), bf16),
            pltpu.VMEM((4, members, group_rows, width), bf16),
            pltpu.VMEM((4, members, group_rows, width), bf16),
            pltpu.VMEM((4, groups, PAD, width), bf16),
            pltpu.VMEM((4, groups, PAD, width), bf16),
            pltpu.VMEM((4 * flat, 128), f32),
            pltpu.VMEM((SAMPLES, 4 * flat, 128), f32),
            pltpu.VMEM((keys, 4 * flat, 128), f32),
            pltpu.SemaphoreType.DMA((4, 4)),
            pltpu.SemaphoreType.DMA((4, 4)),
            pltpu.SemaphoreType.DMA((7,)),
            pltpu.SemaphoreType.DMA((9,)),
            pltpu.SemaphoreType.DMA((9,)),
        ],
        compiler_params=pltpu.CompilerParams(has_side_effects=True, vmem_limit_bytes=58 * 1024 * 1024),
        name="flow_step",
    )(
        hidden,
        own.reshape(2, flat, 128),
        jnp.tile(w_final, (1, 128 // patch)),
        choice,
        spread,
        modulation,
        jnp.repeat(router[0], PAD, axis=1),
        w_in,
        w_out,
    )
    return (
        next_flat.reshape(2, rows, patch),
        mean_flat.reshape(prompts, SEQ, patch),
        var_flat.reshape(prompts, SEQ, patch),
    )


def solution(mesh):
    placed = (
        P(None, "expert", None),
        P(),
        P(),
        P("segment", None, None, None),
        P("segment", None, None),
        P("segment", "expert", None, None),
        P("segment", "expert", None, None),
        P("segment", None, "expert", None),
        P(),
    )
    return jax.shard_map(
        local,
        mesh=mesh,
        in_specs=placed,
        out_specs=(P("segment", "expert", None), P(), P()),
        check_vma=False,
    )
```

```python
import functools

import jax
import jax.numpy as jnp
from jax import lax
from jax.experimental import pallas as pl
from jax.experimental.pallas import tpu as pltpu
from jax.sharding import PartitionSpec as P

SAMPLES = 8
SEQ = 256
CAP = 5
PAD = 8
Z_FIRST = 640

epsilon = 1e-06
time_step = 0.25
time_left = 0.5

f32 = jnp.float32
bf16 = jnp.bfloat16
MESH = pl.DeviceIdType.MESH


def normalize(values_in):
    centered = values_in - jnp.mean(values_in, axis=-1, keepdims=True)
    variance = jnp.mean(centered * centered, axis=-1, keepdims=True)
    return centered * lax.rsqrt(variance + epsilon)


def dot(left, right, over_left=1, over_right=0, **kwargs):
    dims = (((over_left,), (over_right,)), ((), ()))
    return lax.dot_general(left, right, dims, preferred_element_type=f32, **kwargs)


def iota(shape, dim):
    return lax.broadcasted_iota(jnp.int32, shape, dim)


def kernel(
    sizes,
    latents, cond, w_embed, modulation, router_in, w_first, w_second, routes_in, w_final,
    next_out, mean_out, var_out,
    hid, mix, routes, mods, router, first, second,
    out_send, out_recv, rows_in, rows_out, pair_recv, pair_send, own_recv, line_recv, line_send, cross_recv,
    home_send, home_recv, stats, stats_recv, maps,
    send_sems, recv_sems, load_sems, push_sems, land_sems, map_sems,
):
    groups, members, samples, rows, width, cut = sizes
    half = members // 2
    group_rows = groups * CAP
    slots = groups * PAD
    halves = groups // samples
    keys = 2 * halves * members
    core = lax.axis_index("segment")
    device = lax.axis_index("expert")
    group, member = device // members, device % members
    prompt_half, sample = group // samples, group % samples
    plane, place = member // half, member % half
    far_plane = 1 - plane
    other = 1 - core
    key = (core * halves + prompt_half) * members + member

    def expert_at(to_group, to_member):
        return {"expert": to_group * members + to_member}

    def in_group(to_plane, to_place):
        return expert_at(group, to_plane * half + to_place)

    def key_device(to_key):
        to_core = to_key // (halves * members)
        to_half = (to_key // members) % halves
        return {"segment": to_core, "expert": (to_half * samples + sample) * members + to_key % members}

    left, right = (place + half - 1) % half, (place + 1) % half

    barrier = pltpu.get_barrier_semaphore()

    @pl.loop(1, groups)
    def _(k):
        pl.semaphore_signal(
            barrier, inc=1, device_id=expert_at((group + k) % groups, member), device_id_type=MESH
        )

    @pl.loop(1, members)
    def _(k):
        pl.semaphore_signal(
            barrier, inc=1, device_id=expert_at(group, (member + k) % members), device_id_type=MESH
        )

    @pl.loop(1, keys)
    def _(k):
        pl.semaphore_signal(barrier, inc=1, device_id=key_device((key + k) % keys), device_id_type=MESH)

    def load_pairs(micro_core):
        return [
            (routes_in.at[pl.ds(2 * micro_core, 2)], routes.at[core]),
            (router_in, router.at[core]),
            (modulation, mods.at[core]),
            (w_first.at[0, 0], first.at[core]),
            (w_second.at[0, 0], second.at[core]),
        ]

    own_loads = [
        pltpu.make_async_copy(src, dst, load_sems.at[i]) for i, (src, dst) in enumerate(load_pairs(core))
    ]
    pushes = [
        pltpu.make_async_remote_copy(
            src_ref=src, dst_ref=dst, send_sem=push_sems.at[i], recv_sem=land_sems.at[i],
            device_id={"segment": other}, device_id_type=MESH,
        )
        for i, (src, dst) in enumerate(load_pairs(other))
    ]
    for copy in own_loads:
        copy.start()

    frequency = jnp.exp(
        -jnp.log(jnp.full((1, width // 2), 10000.0, f32))
        * iota((1, width // 2), 1).astype(f32) / (width // 2)
    )
    position = (member * rows + iota((rows, 1), 0)).astype(f32)
    angles = position * frequency
    table = jnp.concatenate([jnp.sin(angles), jnp.cos(angles)], axis=1)
    for micro in range(2):
        prompt = (2 * core + micro) * halves + prompt_half
        embedded = dot(latents[2 * core + micro].T, w_embed[...], precision=lax.Precision.HIGHEST)
        hid[micro] = (embedded + table + cond[pl.ds(prompt, 1)]).astype(bf16)

    def packing(shape, row_dim):
        row, slot = iota(shape, row_dim), iota(shape, 1 - row_dim)
        within = slot & (PAD - 1)
        return jnp.where((row == CAP * (slot >> 3) + within) & (within < CAP), 1.0, 0.0).astype(bf16)

    def wait_bytes(ref, sem):
        pltpu.make_async_copy(ref, ref, sem).wait()

    def send(source, target, send_sem, recv_sem, to):
        pltpu.make_async_remote_copy(
            src_ref=source, dst_ref=target, send_sem=send_sem, recv_sem=recv_sem,
            device_id=to, device_id_type=MESH,
        ).start()

    def send_across(unit, source, target, send_sem, recv_sem):
        target[unit, group] = source[unit, group]

        @pl.loop(1, groups)
        def _(k):
            to_group = (group + k) % groups
            send(
                source.at[unit, to_group], target.at[unit, group], send_sem, recv_sem,
                expert_at(to_group, member),
            )

    def front(layer, micro):
        unit = 2 * layer + micro
        prompt = (2 * core + micro) * halves + prompt_half
        shift, scale = mods[layer, 0, pl.ds(prompt, 1)], mods[layer, 1, pl.ds(prompt, 1)]
        normed = (normalize(hid[micro].astype(f32)) * (1.0 + scale) + shift).astype(bf16)
        logits = dot(router[layer], normed, 1, 1)
        chosen = routes[layer, micro]
        expert = iota((groups, rows), 0)
        slot = iota((slots, rows), 0)
        probs, hots = [], []
        for k in range(2):
            picked = jnp.sum(jnp.where(expert == chosen[k : k + 1], logits, 0.0), axis=0, keepdims=True)
            probs.append(lax.logistic(picked))
            hots.append((slot >> 3) == chosen[k : k + 1])
        both = jnp.where(hots[0] | hots[1], 1.0, 0.0)
        earlier = jnp.where(iota((rows, rows), 0) < iota((rows, rows), 1), 1.0, 0.0).astype(bf16)
        before = dot(both.astype(bf16), earlier)
        match = jnp.where(before == (slot & (PAD - 1)).astype(f32), 1.0, 0.0)
        mix[micro] = (
            jnp.where(hots[0], match, 0.0) * probs[0] + jnp.where(hots[1], match, 0.0) * probs[1]
        ) / (probs[0] + probs[1])
        packed = dot((both * match).astype(bf16), normed)
        out_send[unit] = packed.reshape(groups, PAD, width).astype(bf16)
        send_across(unit, out_send, out_recv, send_sems.at[0, unit], recv_sems.at[0, unit])

    half_width = width // 2

    def gather(layer, micro):
        unit = 2 * layer + micro
        wait_bytes(out_recv.at[unit, pl.ds(0, groups - 1)], recv_sems.at[0, unit])
        arrived = out_recv[unit].astype(f32).reshape(slots, width).astype(bf16)
        rows_in[unit, plane, place] = dot(packing((group_rows, slots), 0), arrived).astype(bf16)
        block = rows_in.at[unit, plane, place]
        send(block, block, send_sems.at[1, unit], recv_sems.at[1, unit], in_group(far_plane, place))
        send(block, block, send_sems.at[1, unit], recv_sems.at[2, unit], in_group(plane, right))
        send(block, block, send_sems.at[1, unit], recv_sems.at[3, unit], in_group(plane, left))

    def relay_across(layer, micro):
        unit = 2 * layer + micro
        block = rows_in.at[unit, far_plane, place]
        wait_bytes(block, recv_sems.at[1, unit])
        send(block, block, send_sems.at[7, unit], recv_sems.at[4, unit], in_group(plane, right))
        send(block, block, send_sems.at[7, unit], recv_sems.at[5, unit], in_group(plane, left))

    def relay_along(unit, of_plane, sem):
        from_left = rows_in.at[unit, of_plane, left]
        from_right = rows_in.at[unit, of_plane, right]
        wait_bytes(from_left, recv_sems.at[sem, unit])
        low = rows_in.at[unit, of_plane, left, :, pl.ds(0, half_width)]
        send(low, low, send_sems.at[7, unit], recv_sems.at[sem + 4, unit], in_group(plane, right))
        wait_bytes(from_right, recv_sems.at[sem + 1, unit])
        high = rows_in.at[unit, of_plane, right, :, pl.ds(half_width, half_width)]
        send(high, high, send_sems.at[7, unit], recv_sems.at[sem + 4, unit], in_group(plane, left))

    def expert(unit, layer, of_plane):
        inner = dot(rows_in[unit, of_plane].reshape(half * group_rows, width), first[layer])
        inner = jax.nn.gelu(inner, approximate=True).astype(bf16)
        partial = dot(inner, second[layer]).astype(bf16)
        rows_out[unit, of_plane] = partial.reshape(half, group_rows, width)

        @pl.loop(1, half)
        def _(k):
            to_place = (place + k) % half
            send(
                rows_out.at[unit, of_plane, to_place, :, pl.ds(cut, width - cut)],
                line_recv.at[unit, place, of_plane],
                send_sems.at[3, unit], recv_sems.at[9, unit], in_group(plane, to_place),
            )

    def compute(layer, micro):
        unit = 2 * layer + micro
        wait_bytes(rows_in.at[unit, far_plane, 0], recv_sems.at[8, unit])

        @pl.loop(0, 2)
        def _(step):
            @pl.when(step == 1)
            def _():
                send(
                    rows_out.at[unit, far_plane, :, :, pl.ds(0, cut)], pair_recv.at[unit],
                    send_sems.at[2, unit], recv_sems.at[7, unit], in_group(far_plane, place),
                )
                wait_bytes(rows_in.at[unit, plane, 0], recv_sems.at[6, unit])

            expert(unit, layer, (far_plane + step) % 2)

        for of_plane in range(2):
            line_recv[unit, place, of_plane] = rows_out[unit, of_plane, place, :, pl.ds(cut, width - cut)]

    def reduce_pair(layer, micro):
        unit = 2 * layer + micro
        wait_bytes(pair_recv.at[unit], recv_sems.at[7, unit])

        @pl.loop(0, half)
        def _(k):
            to_place = (place + 1 + k) % half
            mine = rows_out[unit, plane, to_place, :, pl.ds(0, cut)].astype(f32)
            pair_send[unit, to_place] = (mine + pair_recv[unit, to_place].astype(f32)).astype(bf16)

            @pl.when(k < half - 1)
            def _():
                send(
                    pair_send.at[unit, to_place], own_recv.at[unit, place],
                    send_sems.at[4, unit], recv_sems.at[10, unit], in_group(plane, to_place),
                )

        own_recv[unit, place] = pair_send[unit, place]

    def line_total(unit, of_plane):
        total = line_recv[unit, 0, of_plane].astype(f32)
        for k in range(1, half):
            total = total + line_recv[unit, k, of_plane].astype(f32)
        return total

    def reduce_line(layer, micro):
        unit = 2 * layer + micro
        wait_bytes(line_recv.at[unit, pl.ds(0, half - 1)], recv_sems.at[9, unit])
        line_send[unit] = line_total(unit, far_plane).astype(bf16)
        send(
            line_send.at[unit], cross_recv.at[unit],
            send_sems.at[5, unit], recv_sems.at[11, unit], in_group(far_plane, place),
        )

    def send_home(layer, micro):
        unit = 2 * layer + micro
        wait_bytes(own_recv.at[unit, pl.ds(0, half - 1)], recv_sems.at[10, unit])
        total = own_recv[unit, 0].astype(f32)
        for k in range(1, half):
            total = total + own_recv[unit, k].astype(f32)
        line = line_total(unit, plane)
        wait_bytes(cross_recv.at[unit], recv_sems.at[11, unit])
        line = line + cross_recv[unit].astype(f32)
        unpacking = packing((slots, group_rows), 1)
        spaced = dot(unpacking, jnp.concatenate([total.astype(bf16), line.astype(bf16)], axis=1))
        home_send[unit] = spaced.reshape(groups, PAD, width).astype(bf16)
        send_across(unit, home_send, home_recv, send_sems.at[6, unit], recv_sems.at[12, unit])

    def combine(layer, micro):
        unit = 2 * layer + micro
        wait_bytes(home_recv.at[unit, pl.ds(0, groups - 1)], recv_sems.at[12, unit])
        returned = home_recv[unit].astype(f32).reshape(slots, width).astype(bf16)
        weights = mix[micro].T
        coarse = weights.astype(bf16)
        fine = (weights - coarse.astype(f32)).astype(bf16)
        moe = dot(coarse, returned) + dot(fine, returned)
        prompt = (2 * core + micro) * halves + prompt_half
        gate = mods[layer, 2, pl.ds(prompt, 1)]
        hid[micro] = (hid[micro].astype(f32) + gate * moe).astype(bf16)

    pl.semaphore_wait(barrier, groups - 1 + members - 1 + keys - 1)
    for copy in pushes:
        copy.start()

    for copy in own_loads[:3]:
        copy.wait()
    for copy in pushes[:3]:
        copy.wait_recv()

    for micro in range(2):
        front(0, micro)

    @pl.loop(0, 2)
    def _(layer):
        @pl.loop(0, 2)
        def _(micro):
            gather(layer, micro)

        @pl.loop(0, 2)
        def _(micro):
            relay_across(layer, micro)

        @pl.loop(0, 2)
        def _(micro):
            relay_along(2 * layer + micro, plane, 2)

        @pl.loop(0, 2)
        def _(micro):
            relay_along(2 * layer + micro, far_plane, 4)

        @pl.when(layer == 0)
        def _():
            for copy in own_loads[3:]:
                copy.wait()
            for copy in pushes[3:]:
                copy.wait_recv()

        @pl.loop(0, 2)
        def _(micro):
            compute(layer, micro)

        @pl.loop(0, 2)
        def _(micro):
            reduce_pair(layer, micro)
            reduce_line(layer, micro)

        @pl.loop(0, 2)
        def _(micro):
            send_home(layer, micro)

        @pl.loop(0, 2)
        def _(micro):
            combine(layer, micro)

            @pl.when(layer == 0)
            def _():
                front(1, micro)

    pieces = []
    for micro in range(2):
        final = normalize(hid[micro].astype(f32)).astype(bf16)
        velocity = dot(w_final[...], final, 1, 1)
        start = latents[2 * core + micro]
        next_out[micro] = start + time_step * velocity
        clean = start + time_left * velocity
        pieces += [clean, clean * clean]
    stats[...] = jnp.concatenate(pieces, axis=1)
    stats_recv[sample] = stats[...]

    @pl.loop(1, samples)
    def _(k):
        to_sample = (sample + k) % samples
        send(
            stats, stats_recv.at[sample], map_sems.at[0], map_sems.at[1],
            expert_at(prompt_half * samples + to_sample, member),
        )

    wait_bytes(stats_recv.at[pl.ds(0, samples - 1)], map_sems.at[1])
    total = stats_recv[0]
    for k in range(1, samples):
        total = total + stats_recv[k]
    maps[key] = total

    @pl.loop(1, keys)
    def _(k):
        send(maps.at[key], maps.at[key], map_sems.at[2], map_sems.at[3], key_device((key + k) % keys))

    wait_bytes(maps.at[pl.ds(0, keys - 1)], map_sems.at[3])
    for from_core in range(2):
        for from_half in range(halves):
            blocks = [maps[(from_core * halves + from_half) * members + k] for k in range(members)]
            for micro in range(2):
                prompt = (2 * from_core + micro) * halves + from_half
                lanes = [slice((2 * micro + i) * rows, (2 * micro + i + 1) * rows) for i in range(2)]
                mean = jnp.concatenate([block[:, lanes[0]] for block in blocks], axis=1) / SAMPLES
                square = jnp.concatenate([block[:, lanes[1]] for block in blocks], axis=1) / SAMPLES
                mean_out[prompt] = mean
                var_out[prompt] = square - mean * mean

    for copy in pushes:
        copy.wait_send()
    wait_bytes(stats_recv.at[pl.ds(0, samples - 1)], map_sems.at[0])
    wait_bytes(maps.at[pl.ds(0, keys - 1)], map_sems.at[2])

    @pl.loop(0, 4)
    def _(unit):
        wait_bytes(out_recv.at[unit, pl.ds(0, groups - 1)], send_sems.at[0, unit])
        wait_bytes(out_recv.at[unit, pl.ds(0, groups - 1)], send_sems.at[6, unit])
        wait_bytes(rows_in.at[unit, 0], send_sems.at[7, unit])
        wait_bytes(rows_in.at[unit, 0, pl.ds(0, half - 1)], send_sems.at[1, unit])
        wait_bytes(pair_recv.at[unit], send_sems.at[2, unit])
        wait_bytes(line_recv.at[unit, pl.ds(0, half - 1)], send_sems.at[3, unit])
        wait_bytes(own_recv.at[unit, pl.ds(0, half - 1)], send_sems.at[4, unit])
        wait_bytes(line_send.at[unit], send_sems.at[5, unit])


def local(latents, cond, w_embed, modulation, router, w_in, w_out, routes, w_final):
    devices = lax.axis_size("expert")
    rows, patch = latents.shape[1], latents.shape[2]
    width, groups = router.shape[1], router.shape[2]
    hidden_slice = w_in.shape[3]
    members = devices // groups
    half = members // 2
    slots = groups * PAD
    group_rows = groups * CAP
    prompts = cond.shape[0]
    keys = 2 * (groups // SAMPLES) * members

    vmem = pl.BlockSpec(memory_space=pltpu.VMEM)
    left = pl.BlockSpec(memory_space=pl.ANY)
    sizes = (groups, members, SAMPLES, rows, width, Z_FIRST)
    next_rows, mean_map, var_map = pl.pallas_call(
        functools.partial(kernel, sizes),
        out_shape=(
            jax.ShapeDtypeStruct((2, patch, rows), f32),
            jax.ShapeDtypeStruct((prompts, patch, members * rows), f32),
            jax.ShapeDtypeStruct((prompts, patch, members * rows), f32),
        ),
        in_specs=[vmem, vmem, vmem, left, left, left, left, vmem, vmem],
        out_specs=(vmem, vmem, vmem),
        scratch_shapes=[
            pltpu.VMEM((2, rows, width), bf16),
            pltpu.VMEM((2, slots, rows), f32),
            pltpu.VMEM((2, 2, 2, rows), jnp.int32),
            pltpu.VMEM((2, 3, prompts, width), f32),
            pltpu.VMEM((2, groups, width), bf16),
            pltpu.VMEM((2, width, hidden_slice), bf16),
            pltpu.VMEM((2, hidden_slice, width), bf16),
            pltpu.VMEM((4, groups, PAD, width), bf16),
            pltpu.VMEM((4, groups, PAD, width), bf16),
            pltpu.VMEM((4, 2, half, group_rows, width), bf16),
            pltpu.VMEM((4, 2, half, group_rows, width), bf16),
            pltpu.VMEM((4, half, group_rows, Z_FIRST), bf16),
            pltpu.VMEM((4, half, group_rows, Z_FIRST), bf16),
            pltpu.VMEM((4, half, group_rows, Z_FIRST), bf16),
            pltpu.VMEM((4, half, 2, group_rows, width - Z_FIRST), bf16),
            pltpu.VMEM((4, group_rows, width - Z_FIRST), bf16),
            pltpu.VMEM((4, group_rows, width - Z_FIRST), bf16),
            pltpu.VMEM((4, groups, PAD, width), bf16),
            pltpu.VMEM((4, groups, PAD, width), bf16),
            pltpu.VMEM((patch, 4 * rows), f32),
            pltpu.VMEM((SAMPLES, patch, 4 * rows), f32),
            pltpu.VMEM((keys, patch, 4 * rows), f32),
            pltpu.SemaphoreType.DMA((8, 4)),
            pltpu.SemaphoreType.DMA((13, 4)),
            pltpu.SemaphoreType.DMA((5,)),
            pltpu.SemaphoreType.DMA((5,)),
            pltpu.SemaphoreType.DMA((5,)),
            pltpu.SemaphoreType.DMA((4,)),
        ],
        compiler_params=pltpu.CompilerParams(
            has_side_effects=True, collective_id=0, vmem_limit_bytes=58 * 1024 * 1024
        ),
        name="flow_step",
    )(
        latents.transpose(0, 2, 1),
        cond,
        w_embed,
        modulation[0].transpose(1, 0, 2),
        router[0].T,
        w_in,
        w_out,
        routes[0].transpose(0, 2, 1),
        w_final.T,
    )
    return (next_rows.transpose(0, 2, 1), mean_map.transpose(0, 2, 1), var_map.transpose(0, 2, 1))


def solution(mesh):
    placed = (
        P(None, "expert", None),
        P(),
        P(),
        P("segment", None, None, None),
        P("segment", None, None),
        P("segment", "expert", None, None),
        P("segment", "expert", None, None),
        P("segment", None, "expert", None),
        P(),
    )
    return jax.shard_map(
        local,
        mesh=mesh,
        in_specs=placed,
        out_specs=(P("segment", "expert", None), P(), P()),
        check_vma=False,
    )
```

```python
import functools

import jax
import jax.numpy as jnp
from jax import lax
from jax.experimental import pallas as pl
from jax.experimental.pallas import tpu as pltpu
from jax.sharding import PartitionSpec as P

SAMPLES = 8
SEQ = 256
CAP = 5
PAD = 8
Z_FIRST = 896
ALONG_Y = 1024

epsilon = 1e-06
time_step = 0.25
time_left = 0.5

f32 = jnp.float32
bf16 = jnp.bfloat16
MESH = pl.DeviceIdType.MESH


def normalize(values_in):
    centered = values_in - jnp.mean(values_in, axis=-1, keepdims=True)
    variance = jnp.mean(centered * centered, axis=-1, keepdims=True)
    return centered * lax.rsqrt(variance + epsilon)


def dot(left, right, over_left=1, over_right=0, **kwargs):
    dims = (((over_left,), (over_right,)), ((), ()))
    return lax.dot_general(left, right, dims, preferred_element_type=f32, **kwargs)


def iota(shape, dim):
    return lax.broadcasted_iota(jnp.int32, shape, dim)


def kernel(
    sizes,
    latents, cond, w_embed, modulation, router_in, w_first, w_second, routes_in, w_final,
    next_out, maps_out,
    hid, mix, routes, mods, router, first, second,
    out_send, out_recv, rows_in, rows_out, pair_recv, pair_send, own_recv, line_recv, line_send, cross_recv,
    home_send, home_recv, stats, stats_recv, maps,
    send_sems, recv_sems, load_sems, push_sems, land_sems, map_sems,
):
    groups, members, samples, rows, width, cut, along = sizes
    half = members // 2
    group_rows = groups * CAP
    slots = groups * PAD
    halves = groups // samples
    keys = 2 * halves * members
    core = lax.axis_index("segment")
    device = lax.axis_index("expert")
    group, member = device // members, device % members
    prompt_half, sample = group // samples, group % samples
    plane, place = member // half, member % half
    far_plane = 1 - plane
    other = 1 - core
    key = (core * halves + prompt_half) * members + member

    def expert_at(to_group, to_member):
        return {"expert": to_group * members + to_member}

    def in_group(to_plane, to_place):
        return expert_at(group, to_plane * half + to_place)

    def key_device(to_key):
        to_core = to_key // (halves * members)
        to_half = (to_key // members) % halves
        return {"segment": to_core, "expert": (to_half * samples + sample) * members + to_key % members}

    left, right = (place + half - 1) % half, (place + 1) % half

    barrier = pltpu.get_barrier_semaphore()

    @pl.loop(1, groups)
    def _(k):
        pl.semaphore_signal(
            barrier, inc=1, device_id=expert_at((group + k) % groups, member), device_id_type=MESH
        )

    @pl.loop(1, members)
    def _(k):
        pl.semaphore_signal(
            barrier, inc=1, device_id=expert_at(group, (member + k) % members), device_id_type=MESH
        )

    @pl.loop(1, keys)
    def _(k):
        pl.semaphore_signal(barrier, inc=1, device_id=key_device((key + k) % keys), device_id_type=MESH)

    def load_pairs(micro_core):
        return [
            (routes_in.at[pl.ds(2 * micro_core, 2)], routes.at[core]),
            (router_in, router.at[core]),
            (modulation, mods.at[core]),
            (w_first.at[0, 0], first.at[core]),
            (w_second.at[0, 0], second.at[core]),
        ]

    own_loads = [
        pltpu.make_async_copy(src, dst, load_sems.at[i]) for i, (src, dst) in enumerate(load_pairs(core))
    ]
    pushes = [
        pltpu.make_async_remote_copy(
            src_ref=src, dst_ref=dst, send_sem=push_sems.at[i], recv_sem=land_sems.at[i],
            device_id={"segment": other}, device_id_type=MESH,
        )
        for i, (src, dst) in enumerate(load_pairs(other))
    ]
    for copy in own_loads:
        copy.start()

    frequency = jnp.exp(
        -jnp.log(jnp.full((1, width // 2), 10000.0, f32))
        * iota((1, width // 2), 1).astype(f32) / (width // 2)
    )
    position = (member * rows + iota((rows, 1), 0)).astype(f32)
    angles = position * frequency
    table = jnp.concatenate([jnp.sin(angles), jnp.cos(angles)], axis=1)
    for micro in range(2):
        prompt = (2 * core + micro) * halves + prompt_half
        embedded = dot(latents[2 * core + micro].T, w_embed[...], precision=lax.Precision.HIGHEST)
        hid[micro] = (embedded + table + cond[pl.ds(prompt, 1)]).astype(bf16)

    seg = width // 6
    half_width = width // 2

    def packing(shape, row_dim, part):
        row, slot = iota(shape, row_dim), iota(shape, 1 - row_dim)
        within, start = slot & (PAD - 1), CAP * (slot >> 3)
        if part < 2:
            hit = (row == start + (within & 3)) & ((within >> 2) == part)
        else:
            hit = (row == start + 4) & (within == part - 2)
        return jnp.where(hit, 1.0, 0.0).astype(bf16)

    def unpack_rows(low, last, matrix):
        parts = []
        for h in range(2):
            tail = jnp.concatenate([dot(matrix(2 + 3 * h + i), last) for i in range(3)], axis=1)
            parts.append(dot(matrix(h), low) + tail)
        return parts

    def pack_rows(full, matrix):
        low = dot(matrix(0), full[:, :half_width]) + dot(matrix(1), full[:, half_width:])
        last = dot(matrix(2), full[:, :seg])
        for i in range(1, 6):
            last = last + dot(matrix(2 + i), full[:, i * seg : (i + 1) * seg])
        return jnp.concatenate([low, last], axis=1).reshape(groups, PAD, 4 * seg).astype(bf16)

    def blocks_of(ref, unit):
        arrived = ref[unit].astype(f32).reshape(slots, 4 * seg).astype(bf16)
        return arrived[:, :half_width], arrived[:, half_width:]

    def wait_bytes(ref, sem):
        pltpu.make_async_copy(ref, ref, sem).wait()

    def send(source, target, send_sem, recv_sem, to):
        pltpu.make_async_remote_copy(
            src_ref=source, dst_ref=target, send_sem=send_sem, recv_sem=recv_sem,
            device_id=to, device_id_type=MESH,
        ).start()

    def send_across(unit, source, target, send_sem, recv_sem):
        target[unit, group] = source[unit, group]

        @pl.loop(1, groups)
        def _(k):
            to_group = (group + k) % groups
            send(
                source.at[unit, to_group], target.at[unit, group], send_sem, recv_sem,
                expert_at(to_group, member),
            )

    def front(layer, micro):
        unit = 2 * layer + micro
        prompt = (2 * core + micro) * halves + prompt_half
        shift, scale = mods[layer, 0, pl.ds(prompt, 1)], mods[layer, 1, pl.ds(prompt, 1)]
        normed = (normalize(hid[micro].astype(f32)) * (1.0 + scale) + shift).astype(bf16)
        logits = dot(router[layer], normed, 1, 1)
        chosen = routes[layer, micro]
        expert = iota((groups, rows), 0)
        slot = iota((slots, rows), 0)
        probs, hots = [], []
        for k in range(2):
            picked = jnp.sum(jnp.where(expert == chosen[k : k + 1], logits, 0.0), axis=0, keepdims=True)
            probs.append(lax.logistic(picked))
            hots.append((slot >> 3) == chosen[k : k + 1])
        both = jnp.where(hots[0] | hots[1], 1.0, 0.0)
        earlier = jnp.where(iota((rows, rows), 0) < iota((rows, rows), 1), 1.0, 0.0).astype(bf16)
        before = dot(both.astype(bf16), earlier)
        within = slot & (PAD - 1)
        mix[micro, 0] = (
            jnp.where(hots[0], probs[0], 0.0) + jnp.where(hots[1], probs[1], 0.0)
        ) / (probs[0] + probs[1])
        mix[micro, 1] = before

        def spread(part):
            if part < 2:
                hit = (before == (within & 3).astype(f32)) & ((within >> 2) == part)
            else:
                hit = (before == 4.0) & (within == part - 2)
            return jnp.where(hit, both, 0.0).astype(bf16)

        out_send[unit] = pack_rows(normed, spread)
        send_across(unit, out_send, out_recv, send_sems.at[0, unit], recv_sems.at[0, unit])

    def gather(layer, micro):
        unit = 2 * layer + micro
        wait_bytes(out_recv.at[unit, pl.ds(0, groups - 1)], recv_sems.at[0, unit])
        parts = unpack_rows(*blocks_of(out_recv, unit), lambda part: packing((group_rows, slots), 0, part))
        for h in range(2):
            rows_in[unit, plane, place, :, pl.ds(h * half_width, half_width)] = parts[h].astype(bf16)
        block = rows_in.at[unit, plane, place]
        send(block, block, send_sems.at[1, unit], recv_sems.at[1, unit], in_group(far_plane, place))
        send(block, block, send_sems.at[1, unit], recv_sems.at[2, unit], in_group(plane, right))
        send(block, block, send_sems.at[1, unit], recv_sems.at[3, unit], in_group(plane, left))

    def relay_across(layer, micro):
        unit = 2 * layer + micro
        wait_bytes(rows_in.at[unit, far_plane, place], recv_sems.at[1, unit])
        block = rows_in.at[unit, far_plane, place, :, pl.ds(0, along)]
        send(block, block, send_sems.at[7, unit], recv_sems.at[4, unit], in_group(plane, right))
        send(block, block, send_sems.at[7, unit], recv_sems.at[5, unit], in_group(plane, left))

    def cross(unit, from_place):
        block = rows_in.at[unit, plane, from_place, :, pl.ds(along, width - along)]
        send(block, block, send_sems.at[7, unit], recv_sems.at[13, unit], in_group(far_plane, place))

    def relay_own(layer, micro):
        unit = 2 * layer + micro
        wait_bytes(rows_in.at[unit, plane, left], recv_sems.at[2, unit])
        low = rows_in.at[unit, plane, left, :, pl.ds(0, half_width)]
        send(low, low, send_sems.at[7, unit], recv_sems.at[6, unit], in_group(plane, right))
        cross(unit, left)
        wait_bytes(rows_in.at[unit, plane, right], recv_sems.at[3, unit])
        high = rows_in.at[unit, plane, right, :, pl.ds(half_width, half_width)]
        send(high, high, send_sems.at[7, unit], recv_sems.at[6, unit], in_group(plane, left))
        cross(unit, right)

    def relay_far(layer, micro):
        unit = 2 * layer + micro
        wait_bytes(rows_in.at[unit, far_plane, left, :, pl.ds(0, along)], recv_sems.at[4, unit])
        low = rows_in.at[unit, far_plane, left, :, pl.ds(0, along // 2)]
        send(low, low, send_sems.at[7, unit], recv_sems.at[8, unit], in_group(plane, right))
        wait_bytes(rows_in.at[unit, far_plane, right, :, pl.ds(0, along)], recv_sems.at[5, unit])
        high = rows_in.at[unit, far_plane, right, :, pl.ds(along // 2, along // 2)]
        send(high, high, send_sems.at[7, unit], recv_sems.at[8, unit], in_group(plane, left))

    def relay_opposite(layer, micro):
        unit = 2 * layer + micro
        wait_bytes(rows_in.at[unit, plane, 0], recv_sems.at[6, unit])
        cross(unit, (place + 2) % half)

    def expert(unit, layer, of_plane):
        inner = dot(rows_in[unit, of_plane].reshape(half * group_rows, width), first[layer])
        inner = jax.nn.gelu(inner, approximate=True).astype(bf16)
        partial = dot(inner, second[layer]).astype(bf16)
        rows_out[unit, of_plane] = partial.reshape(half, group_rows, width)

        @pl.loop(1, half)
        def _(k):
            to_place = (place + k) % half
            send(
                rows_out.at[unit, of_plane, to_place, :, pl.ds(cut, width - cut)],
                line_recv.at[unit, place, of_plane],
                send_sems.at[3, unit], recv_sems.at[9, unit], in_group(plane, to_place),
            )

    def compute(layer, micro):
        unit = 2 * layer + micro

        @pl.loop(0, 2)
        def _(step):
            @pl.when(step == 1)
            def _():
                wait_bytes(rows_in.at[unit, far_plane, 0, :, pl.ds(0, along)], recv_sems.at[8, unit])
                wait_bytes(
                    rows_in.at[unit, far_plane, pl.ds(0, half - 1), :, pl.ds(along, width - along)],
                    recv_sems.at[13, unit],
                )

            expert(unit, layer, (plane + step) % 2)

        send(
            rows_out.at[unit, far_plane, :, :, pl.ds(0, cut)], pair_recv.at[unit],
            send_sems.at[2, unit], recv_sems.at[7, unit], in_group(far_plane, place),
        )
        for of_plane in range(2):
            line_recv[unit, place, of_plane] = rows_out[unit, of_plane, place, :, pl.ds(cut, width - cut)]

    def reduce_pair(layer, micro):
        unit = 2 * layer + micro
        wait_bytes(pair_recv.at[unit], recv_sems.at[7, unit])

        @pl.loop(0, half)
        def _(k):
            to_place = (place + 1 + k) % half
            mine = rows_out[unit, plane, to_place, :, pl.ds(0, cut)].astype(f32)
            pair_send[unit, to_place] = (mine + pair_recv[unit, to_place].astype(f32)).astype(bf16)

            @pl.when(k < half - 1)
            def _():
                send(
                    pair_send.at[unit, to_place], own_recv.at[unit, place],
                    send_sems.at[4, unit], recv_sems.at[10, unit], in_group(plane, to_place),
                )

        own_recv[unit, place] = pair_send[unit, place]

    def line_total(unit, of_plane):
        total = line_recv[unit, 0, of_plane].astype(f32)
        for k in range(1, half):
            total = total + line_recv[unit, k, of_plane].astype(f32)
        return total

    def reduce_line(layer, micro):
        unit = 2 * layer + micro
        wait_bytes(line_recv.at[unit, pl.ds(0, half - 1)], recv_sems.at[9, unit])
        line_send[unit] = line_total(unit, far_plane).astype(bf16)
        send(
            line_send.at[unit], cross_recv.at[unit],
            send_sems.at[5, unit], recv_sems.at[11, unit], in_group(far_plane, place),
        )

    def send_home(layer, micro):
        unit = 2 * layer + micro
        wait_bytes(own_recv.at[unit, pl.ds(0, half - 1)], recv_sems.at[10, unit])
        total = own_recv[unit, 0].astype(f32)
        for k in range(1, half):
            total = total + own_recv[unit, k].astype(f32)
        line = line_total(unit, plane)
        wait_bytes(cross_recv.at[unit], recv_sems.at[11, unit])
        line = line + cross_recv[unit].astype(f32)
        full = jnp.concatenate([total.astype(bf16), line.astype(bf16)], axis=1)
        home_send[unit] = pack_rows(full, lambda part: packing((slots, group_rows), 1, part))
        send_across(unit, home_send, home_recv, send_sems.at[6, unit], recv_sems.at[12, unit])

    def combine(layer, micro):
        unit = 2 * layer + micro
        wait_bytes(home_recv.at[unit, pl.ds(0, groups - 1)], recv_sems.at[12, unit])
        weights, before = mix[micro, 0].T, mix[micro, 1].T
        within = iota((rows, slots), 1) & (PAD - 1)

        def weighing(part):
            if part < 2:
                hit = (before == (within & 3).astype(f32)) & ((within >> 2) == part)
            else:
                hit = (before == 4.0) & (within == part - 2)
            kept = jnp.where(hit, weights, 0.0)
            coarse = kept.astype(bf16).astype(f32)
            return jnp.concatenate([coarse, kept - coarse], axis=0).astype(bf16)

        both = jnp.concatenate(unpack_rows(*blocks_of(home_recv, unit), weighing), axis=1)
        moe = both[:rows] + both[rows:]
        prompt = (2 * core + micro) * halves + prompt_half
        gate = mods[layer, 2, pl.ds(prompt, 1)]
        hid[micro] = (hid[micro].astype(f32) + gate * moe).astype(bf16)

    pl.semaphore_wait(barrier, groups - 1 + members - 1 + keys - 1)
    for copy in pushes:
        copy.start()

    for copy in own_loads[:3]:
        copy.wait()
    for copy in pushes[:3]:
        copy.wait_recv()

    for micro in range(2):
        front(0, micro)

    @pl.loop(0, 2)
    def _(layer):
        @pl.loop(0, 2)
        def _(micro):
            gather(layer, micro)

        @pl.loop(0, 2)
        def _(micro):
            relay_across(layer, micro)

        @pl.loop(0, 2)
        def _(micro):
            relay_own(layer, micro)

        @pl.loop(0, 2)
        def _(micro):
            relay_far(layer, micro)

        @pl.loop(0, 2)
        def _(micro):
            relay_opposite(layer, micro)

        @pl.when(layer == 0)
        def _():
            for copy in own_loads[3:]:
                copy.wait()
            for copy in pushes[3:]:
                copy.wait_recv()

        @pl.loop(0, 2)
        def _(micro):
            compute(layer, micro)

        @pl.loop(0, 2)
        def _(micro):
            reduce_pair(layer, micro)
            reduce_line(layer, micro)

        @pl.loop(0, 2)
        def _(micro):
            send_home(layer, micro)

        @pl.loop(0, 2)
        def _(micro):
            combine(layer, micro)

            @pl.when(layer == 0)
            def _():
                front(1, micro)

    pieces = []
    for micro in range(2):
        final = normalize(hid[micro].astype(f32)).astype(bf16)
        velocity = dot(w_final[...], final, 1, 1)
        start = latents[2 * core + micro]
        next_out[micro] = start + time_step * velocity
        clean = start + time_left * velocity
        pieces += [clean, clean * clean]
    stats[...] = jnp.concatenate(pieces, axis=1)
    stats_recv[sample] = stats[...]

    @pl.loop(1, samples)
    def _(k):
        to_sample = (sample + k) % samples
        send(
            stats, stats_recv.at[sample], map_sems.at[0], map_sems.at[1],
            expert_at(prompt_half * samples + to_sample, member),
        )

    wait_bytes(stats_recv.at[pl.ds(0, samples - 1)], map_sems.at[1])
    total = stats_recv[0]
    for k in range(1, samples):
        total = total + stats_recv[k]
    maps[key] = total

    @pl.loop(1, keys)
    def _(k):
        send(maps.at[key], maps.at[key], map_sems.at[2], map_sems.at[3], key_device((key + k) % keys))

    wait_bytes(maps.at[pl.ds(0, keys - 1)], map_sems.at[3])
    maps_out[...] = maps[...]

    for copy in pushes:
        copy.wait_send()
    wait_bytes(stats_recv.at[pl.ds(0, samples - 1)], map_sems.at[0])
    wait_bytes(maps.at[pl.ds(0, keys - 1)], map_sems.at[2])

    @pl.loop(0, 4)
    def _(unit):
        wait_bytes(out_recv.at[unit, pl.ds(0, groups - 1)], send_sems.at[0, unit])
        wait_bytes(out_recv.at[unit, pl.ds(0, groups - 1)], send_sems.at[6, unit])
        wait_bytes(rows_in.at[unit, 0], send_sems.at[7, unit])
        wait_bytes(rows_in.at[unit, 0, pl.ds(0, half - 1)], send_sems.at[1, unit])
        wait_bytes(pair_recv.at[unit], send_sems.at[2, unit])
        wait_bytes(line_recv.at[unit, pl.ds(0, half - 1)], send_sems.at[3, unit])
        wait_bytes(own_recv.at[unit, pl.ds(0, half - 1)], send_sems.at[4, unit])
        wait_bytes(line_send.at[unit], send_sems.at[5, unit])


def write_out(sizes, maps, next_in, next_out, mean_out, var_out):
    members, halves, rows = sizes
    next_out[...] = next_in[...]
    for core in range(2):
        for half in range(halves):
            blocks = [maps[(core * halves + half) * members + k] for k in range(members)]
            for micro in range(2):
                prompt = (2 * core + micro) * halves + half
                lanes = [slice((2 * micro + i) * rows, (2 * micro + i + 1) * rows) for i in range(2)]
                mean = jnp.concatenate([block[:, lanes[0]] for block in blocks], axis=1) / SAMPLES
                square = jnp.concatenate([block[:, lanes[1]] for block in blocks], axis=1) / SAMPLES
                mean_out[prompt] = mean
                var_out[prompt] = square - mean * mean


def local(latents, cond, w_embed, modulation, router, w_in, w_out, routes, w_final):
    devices = lax.axis_size("expert")
    rows, patch = latents.shape[1], latents.shape[2]
    width, groups = router.shape[1], router.shape[2]
    hidden_slice = w_in.shape[3]
    members = devices // groups
    half = members // 2
    slots = groups * PAD
    group_rows = groups * CAP
    prompts = cond.shape[0]
    keys = 2 * (groups // SAMPLES) * members

    vmem = pl.BlockSpec(memory_space=pltpu.VMEM)
    left = pl.BlockSpec(memory_space=pl.ANY)
    block_lanes = 4 * (width // 6)
    sizes = (groups, members, SAMPLES, rows, width, Z_FIRST, ALONG_Y)
    next_rows, maps = pl.pallas_call(
        functools.partial(kernel, sizes),
        out_shape=(
            jax.ShapeDtypeStruct((2, patch, rows), f32),
            jax.ShapeDtypeStruct((keys, patch, 4 * rows), f32),
        ),
        in_specs=[vmem, vmem, vmem, left, left, left, left, vmem, vmem],
        out_specs=(vmem, vmem),
        scratch_shapes=[
            pltpu.VMEM((2, rows, width), bf16),
            pltpu.VMEM((2, 2, slots, rows), f32),
            pltpu.VMEM((2, 2, 2, rows), jnp.int32),
            pltpu.VMEM((2, 3, prompts, width), f32),
            pltpu.VMEM((2, groups, width), bf16),
            pltpu.VMEM((2, width, hidden_slice), bf16),
            pltpu.VMEM((2, hidden_slice, width), bf16),
            pltpu.VMEM((4, groups, PAD, block_lanes), bf16),
            pltpu.VMEM((4, groups, PAD, block_lanes), bf16),
            pltpu.VMEM((4, 2, half, group_rows, width), bf16),
            pltpu.VMEM((4, 2, half, group_rows, width), bf16),
            pltpu.VMEM((4, half, group_rows, Z_FIRST), bf16),
            pltpu.VMEM((4, half, group_rows, Z_FIRST), bf16),
            pltpu.VMEM((4, half, group_rows, Z_FIRST), bf16),
            pltpu.VMEM((4, half, 2, group_rows, width - Z_FIRST), bf16),
            pltpu.VMEM((4, group_rows, width - Z_FIRST), bf16),
            pltpu.VMEM((4, group_rows, width - Z_FIRST), bf16),
            pltpu.VMEM((4, groups, PAD, block_lanes), bf16),
            pltpu.VMEM((4, groups, PAD, block_lanes), bf16),
            pltpu.VMEM((patch, 4 * rows), f32),
            pltpu.VMEM((SAMPLES, patch, 4 * rows), f32),
            pltpu.VMEM((keys, patch, 4 * rows), f32),
            pltpu.SemaphoreType.DMA((8, 4)),
            pltpu.SemaphoreType.DMA((14, 4)),
            pltpu.SemaphoreType.DMA((5,)),
            pltpu.SemaphoreType.DMA((5,)),
            pltpu.SemaphoreType.DMA((5,)),
            pltpu.SemaphoreType.DMA((4,)),
        ],
        compiler_params=pltpu.CompilerParams(
            has_side_effects=True, collective_id=0, vmem_limit_bytes=58 * 1024 * 1024
        ),
        name="flow_step",
    )(
        latents.transpose(0, 2, 1),
        cond,
        w_embed,
        modulation[0].transpose(1, 0, 2),
        router[0].T,
        w_in,
        w_out,
        routes[0].transpose(0, 2, 1),
        w_final.T,
    )
    next_rows, mean_map, var_map = pl.pallas_call(
        functools.partial(write_out, (members, groups // SAMPLES, rows)),
        out_shape=(
            jax.ShapeDtypeStruct((2, patch, rows), f32),
            jax.ShapeDtypeStruct((prompts, patch, members * rows), f32),
            jax.ShapeDtypeStruct((prompts, patch, members * rows), f32),
        ),
        in_specs=[vmem, vmem],
        out_specs=(vmem, vmem, vmem),
        name="write_out",
    )(maps, next_rows)
    return (next_rows.transpose(0, 2, 1), mean_map.transpose(0, 2, 1), var_map.transpose(0, 2, 1))


def solution(mesh):
    placed = (
        P(None, "expert", None),
        P(),
        P(),
        P("segment", None, None, None),
        P("segment", None, None),
        P("segment", "expert", None, None),
        P("segment", "expert", None, None),
        P("segment", None, "expert", None),
        P(),
    )
    return jax.shard_map(
        local,
        mesh=mesh,
        in_specs=placed,
        out_specs=(P("segment", "expert", None), P(), P()),
        check_vma=False,
    )
```

```python
import functools

import jax
import jax.numpy as jnp
from jax import lax
from jax.experimental import pallas as pl
from jax.experimental.pallas import tpu as pltpu
from jax.sharding import PartitionSpec as P

SAMPLES = 8
SEQ = 256
CAP = 5
PAD = 8
Z_FIRST = 768
ALONG_Y = 1024

epsilon = 1e-06
time_step = 0.25
time_left = 0.5

f32 = jnp.float32
bf16 = jnp.bfloat16
MESH = pl.DeviceIdType.MESH


def normalize(values_in):
    centered = values_in - jnp.mean(values_in, axis=-1, keepdims=True)
    variance = jnp.mean(centered * centered, axis=-1, keepdims=True)
    return centered * lax.rsqrt(variance + epsilon)


def dot(left, right, over_left=1, over_right=0, **kwargs):
    dims = (((over_left,), (over_right,)), ((), ()))
    return lax.dot_general(left, right, dims, preferred_element_type=f32, **kwargs)


def iota(shape, dim):
    return lax.broadcasted_iota(jnp.int32, shape, dim)


def kernel(
    sizes,
    latents, cond, w_embed, modulation, router_in, w_first, w_second, routes_in, w_final,
    next_out, maps_out,
    hid, mix, routes, mods, router, first, second,
    out_send, out_recv, rows_in, rows_out, pair_recv, pair_send, own_recv, line_recv, line_send, cross_recv,
    home_send, home_recv, stats, stats_recv, maps,
    send_sems, recv_sems, load_sems, push_sems, land_sems, map_sems,
):
    groups, members, samples, rows, width, cut, along = sizes
    half = members // 2
    group_rows = groups * CAP
    slots = groups * PAD
    halves = groups // samples
    keys = 2 * halves * members
    core = lax.axis_index("segment")
    device = lax.axis_index("expert")
    group, member = device // members, device % members
    prompt_half, sample = group // samples, group % samples
    plane, place = member // half, member % half
    far_plane = 1 - plane
    other = 1 - core
    key = (core * halves + prompt_half) * members + member

    def expert_at(to_group, to_member):
        return {"expert": to_group * members + to_member}

    def in_group(to_plane, to_place):
        return expert_at(group, to_plane * half + to_place)

    def key_device(to_key):
        to_core = to_key // (halves * members)
        to_half = (to_key // members) % halves
        return {"segment": to_core, "expert": (to_half * samples + sample) * members + to_key % members}

    left, right = (place + half - 1) % half, (place + 1) % half

    barrier = pltpu.get_barrier_semaphore()

    @pl.loop(1, groups)
    def _(k):
        pl.semaphore_signal(
            barrier, inc=1, device_id=expert_at((group + k) % groups, member), device_id_type=MESH
        )

    @pl.loop(1, members)
    def _(k):
        pl.semaphore_signal(
            barrier, inc=1, device_id=expert_at(group, (member + k) % members), device_id_type=MESH
        )

    @pl.loop(1, keys)
    def _(k):
        pl.semaphore_signal(barrier, inc=1, device_id=key_device((key + k) % keys), device_id_type=MESH)

    def load_pairs(micro_core):
        return [
            (routes_in.at[pl.ds(2 * micro_core, 2)], routes.at[core]),
            (router_in, router.at[core]),
            (modulation, mods.at[core]),
            (w_first.at[0, 0], first.at[core]),
            (w_second.at[0, 0], second.at[core]),
        ]

    own_loads = [
        pltpu.make_async_copy(src, dst, load_sems.at[i]) for i, (src, dst) in enumerate(load_pairs(core))
    ]
    pushes = [
        pltpu.make_async_remote_copy(
            src_ref=src, dst_ref=dst, send_sem=push_sems.at[i], recv_sem=land_sems.at[i],
            device_id={"segment": other}, device_id_type=MESH,
        )
        for i, (src, dst) in enumerate(load_pairs(other))
    ]
    for copy in own_loads:
        copy.start()

    frequency = jnp.exp(
        -jnp.log(jnp.full((1, width // 2), 10000.0, f32))
        * iota((1, width // 2), 1).astype(f32) / (width // 2)
    )
    position = (member * rows + iota((rows, 1), 0)).astype(f32)
    angles = position * frequency
    table = jnp.concatenate([jnp.sin(angles), jnp.cos(angles)], axis=1)
    for micro in range(2):
        prompt = (2 * core + micro) * halves + prompt_half
        embedded = dot(latents[2 * core + micro].T, w_embed[...], precision=lax.Precision.HIGHEST)
        hid[micro] = (embedded + table + cond[pl.ds(prompt, 1)]).astype(bf16)

    seg = width // 6
    half_width = width // 2

    def packing(shape, row_dim, part):
        row, slot = iota(shape, row_dim), iota(shape, 1 - row_dim)
        within, start = slot & (PAD - 1), CAP * (slot >> 3)
        if part < 2:
            hit = (row == start + (within & 3)) & ((within >> 2) == part)
        else:
            hit = (row == start + 4) & (within == part - 2)
        return jnp.where(hit, 1.0, 0.0).astype(bf16)

    def unpack_rows(low, last, matrix):
        parts = []
        for h in range(2):
            tail = jnp.concatenate([dot(matrix(2 + 3 * h + i), last) for i in range(3)], axis=1)
            parts.append(dot(matrix(h), low) + tail)
        return parts

    def pack_rows(full, matrix):
        low = dot(matrix(0), full[:, :half_width]) + dot(matrix(1), full[:, half_width:])
        last = dot(matrix(2), full[:, :seg])
        for i in range(1, 6):
            last = last + dot(matrix(2 + i), full[:, i * seg : (i + 1) * seg])
        return jnp.concatenate([low, last], axis=1).reshape(groups, PAD, 4 * seg).astype(bf16)

    def blocks_of(ref, unit):
        arrived = ref[unit].astype(f32).reshape(slots, 4 * seg).astype(bf16)
        return arrived[:, :half_width], arrived[:, half_width:]

    def wait_bytes(ref, sem):
        pltpu.make_async_copy(ref, ref, sem).wait()

    def send(source, target, send_sem, recv_sem, to):
        pltpu.make_async_remote_copy(
            src_ref=source, dst_ref=target, send_sem=send_sem, recv_sem=recv_sem,
            device_id=to, device_id_type=MESH,
        ).start()

    def send_across(unit, source, target, send_sem, recv_sem):
        target[unit, group] = source[unit, group]

        @pl.loop(1, groups)
        def _(k):
            to_group = (group + k) % groups
            send(
                source.at[unit, to_group], target.at[unit, group], send_sem, recv_sem,
                expert_at(to_group, member),
            )

    def front(layer, micro):
        unit = 2 * layer + micro
        prompt = (2 * core + micro) * halves + prompt_half
        shift, scale = mods[layer, 0, pl.ds(prompt, 1)], mods[layer, 1, pl.ds(prompt, 1)]
        normed = (normalize(hid[micro].astype(f32)) * (1.0 + scale) + shift).astype(bf16)
        logits = dot(router[layer], normed, 1, 1)
        chosen = routes[layer, micro]
        expert = iota((groups, rows), 0)
        slot = iota((slots, rows), 0)
        probs, hots = [], []
        for k in range(2):
            picked = jnp.sum(jnp.where(expert == chosen[k : k + 1], logits, 0.0), axis=0, keepdims=True)
            probs.append(lax.logistic(picked))
            hots.append((slot >> 3) == chosen[k : k + 1])
        both = jnp.where(hots[0] | hots[1], 1.0, 0.0)
        earlier = jnp.where(iota((rows, rows), 0) < iota((rows, rows), 1), 1.0, 0.0).astype(bf16)
        before = dot(both.astype(bf16), earlier)
        within = slot & (PAD - 1)
        mix[micro, 0] = (
            jnp.where(hots[0], probs[0], 0.0) + jnp.where(hots[1], probs[1], 0.0)
        ) / (probs[0] + probs[1])
        mix[micro, 1] = before

        def spread(part):
            if part < 2:
                hit = (before == (within & 3).astype(f32)) & ((within >> 2) == part)
            else:
                hit = (before == 4.0) & (within == part - 2)
            return jnp.where(hit, both, 0.0).astype(bf16)

        out_send[unit] = pack_rows(normed, spread)
        send_across(unit, out_send, out_recv, send_sems.at[0, unit], recv_sems.at[0, unit])

    def gather(layer, micro):
        unit = 2 * layer + micro
        wait_bytes(out_recv.at[unit, pl.ds(0, groups - 1)], recv_sems.at[0, unit])
        parts = unpack_rows(*blocks_of(out_recv, unit), lambda part: packing((group_rows, slots), 0, part))
        for h in range(2):
            rows_in[unit, plane, place, :, pl.ds(h * half_width, half_width)] = parts[h].astype(bf16)
        block = rows_in.at[unit, plane, place]
        send(block, block, send_sems.at[1, unit], recv_sems.at[1, unit], in_group(far_plane, place))
        send(block, block, send_sems.at[1, unit], recv_sems.at[2, unit], in_group(plane, right))
        send(block, block, send_sems.at[1, unit], recv_sems.at[3, unit], in_group(plane, left))

    def relay_across(layer, micro):
        unit = 2 * layer + micro
        wait_bytes(rows_in.at[unit, far_plane, place], recv_sems.at[1, unit])
        block = rows_in.at[unit, far_plane, place, :, pl.ds(0, along)]
        send(block, block, send_sems.at[7, unit], recv_sems.at[4, unit], in_group(plane, right))
        send(block, block, send_sems.at[7, unit], recv_sems.at[5, unit], in_group(plane, left))

    def cross(unit, from_place):
        block = rows_in.at[unit, plane, from_place, :, pl.ds(along, width - along)]
        send(block, block, send_sems.at[7, unit], recv_sems.at[13, unit], in_group(far_plane, place))

    def relay_own(layer, micro):
        unit = 2 * layer + micro
        wait_bytes(rows_in.at[unit, plane, left], recv_sems.at[2, unit])
        low = rows_in.at[unit, plane, left, :, pl.ds(0, half_width)]
        send(low, low, send_sems.at[7, unit], recv_sems.at[6, unit], in_group(plane, right))
        cross(unit, left)
        wait_bytes(rows_in.at[unit, plane, right], recv_sems.at[3, unit])
        high = rows_in.at[unit, plane, right, :, pl.ds(half_width, half_width)]
        send(high, high, send_sems.at[7, unit], recv_sems.at[6, unit], in_group(plane, left))
        cross(unit, right)

    def relay_far(layer, micro):
        unit = 2 * layer + micro
        wait_bytes(rows_in.at[unit, far_plane, left, :, pl.ds(0, along)], recv_sems.at[4, unit])
        low = rows_in.at[unit, far_plane, left, :, pl.ds(0, along // 2)]
        send(low, low, send_sems.at[7, unit], recv_sems.at[8, unit], in_group(plane, right))
        wait_bytes(rows_in.at[unit, far_plane, right, :, pl.ds(0, along)], recv_sems.at[5, unit])
        high = rows_in.at[unit, far_plane, right, :, pl.ds(along // 2, along // 2)]
        send(high, high, send_sems.at[7, unit], recv_sems.at[8, unit], in_group(plane, left))

    def relay_opposite(layer, micro):
        unit = 2 * layer + micro
        wait_bytes(rows_in.at[unit, plane, 0], recv_sems.at[6, unit])
        cross(unit, (place + 2) % half)

    def expert(unit, layer, of_plane):
        inner = dot(rows_in[unit, of_plane].reshape(half * group_rows, width), first[layer])
        inner = jax.nn.gelu(inner, approximate=True).astype(bf16)
        partial = dot(inner, second[layer]).astype(bf16)
        rows_out[unit, of_plane] = partial.reshape(half, group_rows, width)

        @pl.loop(1, half)
        def _(k):
            to_place = (place + k) % half
            send(
                rows_out.at[unit, of_plane, to_place, :, pl.ds(cut, width - cut)],
                line_recv.at[unit, place, of_plane],
                send_sems.at[3, unit], recv_sems.at[9, unit], in_group(plane, to_place),
            )

    def compute(layer, micro):
        unit = 2 * layer + micro

        @pl.loop(0, 2)
        def _(step):
            @pl.when(step == 1)
            def _():
                wait_bytes(rows_in.at[unit, far_plane, 0, :, pl.ds(0, along)], recv_sems.at[8, unit])
                wait_bytes(
                    rows_in.at[unit, far_plane, pl.ds(0, half - 1), :, pl.ds(along, width - along)],
                    recv_sems.at[13, unit],
                )

            expert(unit, layer, (plane + step) % 2)

        send(
            rows_out.at[unit, far_plane, :, :, pl.ds(0, cut)], pair_recv.at[unit],
            send_sems.at[2, unit], recv_sems.at[7, unit], in_group(far_plane, place),
        )
        for of_plane in range(2):
            line_recv[unit, place, of_plane] = rows_out[unit, of_plane, place, :, pl.ds(cut, width - cut)]

    def reduce_pair(layer, micro):
        unit = 2 * layer + micro
        wait_bytes(pair_recv.at[unit], recv_sems.at[7, unit])

        @pl.loop(0, half)
        def _(k):
            to_place = (place + 1 + k) % half
            mine = rows_out[unit, plane, to_place, :, pl.ds(0, cut)].astype(f32)
            pair_send[unit, to_place] = (mine + pair_recv[unit, to_place].astype(f32)).astype(bf16)

            @pl.when(k < half - 1)
            def _():
                send(
                    pair_send.at[unit, to_place], own_recv.at[unit, place],
                    send_sems.at[4, unit], recv_sems.at[10, unit], in_group(plane, to_place),
                )

        own_recv[unit, place] = pair_send[unit, place]

    def line_total(unit, of_plane):
        total = line_recv[unit, 0, of_plane].astype(f32)
        for k in range(1, half):
            total = total + line_recv[unit, k, of_plane].astype(f32)
        return total

    def reduce_line(layer, micro):
        unit = 2 * layer + micro
        wait_bytes(line_recv.at[unit, pl.ds(0, half - 1)], recv_sems.at[9, unit])
        line_send[unit] = line_total(unit, far_plane).astype(bf16)
        send(
            line_send.at[unit], cross_recv.at[unit],
            send_sems.at[5, unit], recv_sems.at[11, unit], in_group(far_plane, place),
        )

    def send_home(layer, micro):
        unit = 2 * layer + micro
        wait_bytes(own_recv.at[unit, pl.ds(0, half - 1)], recv_sems.at[10, unit])
        total = own_recv[unit, 0].astype(f32)
        for k in range(1, half):
            total = total + own_recv[unit, k].astype(f32)
        line = line_total(unit, plane)
        wait_bytes(cross_recv.at[unit], recv_sems.at[11, unit])
        line = line + cross_recv[unit].astype(f32)
        full = jnp.concatenate([total.astype(bf16), line.astype(bf16)], axis=1)
        home_send[unit] = pack_rows(full, lambda part: packing((slots, group_rows), 1, part))
        send_across(unit, home_send, home_recv, send_sems.at[6, unit], recv_sems.at[12, unit])

    def combine(layer, micro):
        unit = 2 * layer + micro
        wait_bytes(home_recv.at[unit, pl.ds(0, groups - 1)], recv_sems.at[12, unit])
        weights, before = mix[micro, 0].T, mix[micro, 1].T
        within = iota((rows, slots), 1) & (PAD - 1)

        def weighing(part):
            if part < 2:
                hit = (before == (within & 3).astype(f32)) & ((within >> 2) == part)
            else:
                hit = (before == 4.0) & (within == part - 2)
            kept = jnp.where(hit, weights, 0.0)
            coarse = kept.astype(bf16).astype(f32)
            return jnp.concatenate([coarse, kept - coarse], axis=0).astype(bf16)

        both = jnp.concatenate(unpack_rows(*blocks_of(home_recv, unit), weighing), axis=1)
        moe = both[:rows] + both[rows:]
        prompt = (2 * core + micro) * halves + prompt_half
        gate = mods[layer, 2, pl.ds(prompt, 1)]
        hid[micro] = (hid[micro].astype(f32) + gate * moe).astype(bf16)

    pl.semaphore_wait(barrier, groups - 1 + members - 1 + keys - 1)
    for copy in pushes:
        copy.start()

    for copy in own_loads[:3]:
        copy.wait()
    for copy in pushes[:3]:
        copy.wait_recv()

    for micro in range(2):
        front(0, micro)

    @pl.loop(0, 2)
    def _(layer):
        @pl.loop(0, 2)
        def _(micro):
            gather(layer, micro)

        @pl.loop(0, 2)
        def _(micro):
            relay_across(layer, micro)

        @pl.loop(0, 2)
        def _(micro):
            relay_own(layer, micro)

        @pl.loop(0, 2)
        def _(micro):
            relay_far(layer, micro)

        @pl.loop(0, 2)
        def _(micro):
            relay_opposite(layer, micro)

        @pl.when(layer == 0)
        def _():
            for copy in own_loads[3:]:
                copy.wait()
            for copy in pushes[3:]:
                copy.wait_recv()

        @pl.loop(0, 2)
        def _(micro):
            compute(layer, micro)

        @pl.loop(0, 2)
        def _(micro):
            reduce_pair(layer, micro)
            reduce_line(layer, micro)

        @pl.loop(0, 2)
        def _(micro):
            send_home(layer, micro)

        @pl.loop(0, 2)
        def _(micro):
            combine(layer, micro)

            @pl.when(layer == 0)
            def _():
                front(1, micro)

    pieces = []
    for micro in range(2):
        final = normalize(hid[micro].astype(f32)).astype(bf16)
        velocity = dot(w_final[...], final, 1, 1)
        start = latents[2 * core + micro]
        next_out[micro] = start + time_step * velocity
        clean = start + time_left * velocity
        pieces += [clean, clean * clean]
    stats[...] = jnp.concatenate(pieces, axis=1)
    stats_recv[sample] = stats[...]

    @pl.loop(1, samples)
    def _(k):
        to_sample = (sample + k) % samples
        send(
            stats, stats_recv.at[sample], map_sems.at[0], map_sems.at[1],
            expert_at(prompt_half * samples + to_sample, member),
        )

    wait_bytes(stats_recv.at[pl.ds(0, samples - 1)], map_sems.at[1])
    total = stats_recv[0]
    for k in range(1, samples):
        total = total + stats_recv[k]
    maps[key] = total

    @pl.loop(1, keys)
    def _(k):
        send(maps.at[key], maps.at[key], map_sems.at[2], map_sems.at[3], key_device((key + k) % keys))

    wait_bytes(maps.at[pl.ds(0, keys - 1)], map_sems.at[3])
    maps_out[...] = maps[...]

    for copy in pushes:
        copy.wait_send()
    wait_bytes(stats_recv.at[pl.ds(0, samples - 1)], map_sems.at[0])
    wait_bytes(maps.at[pl.ds(0, keys - 1)], map_sems.at[2])

    @pl.loop(0, 4)
    def _(unit):
        wait_bytes(out_recv.at[unit, pl.ds(0, groups - 1)], send_sems.at[0, unit])
        wait_bytes(out_recv.at[unit, pl.ds(0, groups - 1)], send_sems.at[6, unit])
        wait_bytes(rows_in.at[unit, 0], send_sems.at[7, unit])
        wait_bytes(rows_in.at[unit, 0, pl.ds(0, half - 1)], send_sems.at[1, unit])
        wait_bytes(pair_recv.at[unit], send_sems.at[2, unit])
        wait_bytes(line_recv.at[unit, pl.ds(0, half - 1)], send_sems.at[3, unit])
        wait_bytes(own_recv.at[unit, pl.ds(0, half - 1)], send_sems.at[4, unit])
        wait_bytes(line_send.at[unit], send_sems.at[5, unit])


def write_out(sizes, maps, next_in, next_out, mean_out, var_out):
    members, halves, rows = sizes
    next_out[...] = next_in[...]
    for core in range(2):
        for half in range(halves):
            blocks = [maps[(core * halves + half) * members + k] for k in range(members)]
            for micro in range(2):
                prompt = (2 * core + micro) * halves + half
                lanes = [slice((2 * micro + i) * rows, (2 * micro + i + 1) * rows) for i in range(2)]
                mean = jnp.concatenate([block[:, lanes[0]] for block in blocks], axis=1) / SAMPLES
                square = jnp.concatenate([block[:, lanes[1]] for block in blocks], axis=1) / SAMPLES
                mean_out[prompt] = mean
                var_out[prompt] = square - mean * mean


def local(latents, cond, w_embed, modulation, router, w_in, w_out, routes, w_final):
    devices = lax.axis_size("expert")
    rows, patch = latents.shape[1], latents.shape[2]
    width, groups = router.shape[1], router.shape[2]
    hidden_slice = w_in.shape[3]
    members = devices // groups
    half = members // 2
    slots = groups * PAD
    group_rows = groups * CAP
    prompts = cond.shape[0]
    keys = 2 * (groups // SAMPLES) * members

    vmem = pl.BlockSpec(memory_space=pltpu.VMEM)
    left = pl.BlockSpec(memory_space=pl.ANY)
    block_lanes = 4 * (width // 6)
    sizes = (groups, members, SAMPLES, rows, width, Z_FIRST, ALONG_Y)
    next_rows, maps = pl.pallas_call(
        functools.partial(kernel, sizes),
        out_shape=(
            jax.ShapeDtypeStruct((2, patch, rows), f32),
            jax.ShapeDtypeStruct((keys, patch, 4 * rows), f32),
        ),
        in_specs=[vmem, vmem, vmem, left, left, left, left, vmem, vmem],
        out_specs=(vmem, vmem),
        scratch_shapes=[
            pltpu.VMEM((2, rows, width), bf16),
            pltpu.VMEM((2, 2, slots, rows), f32),
            pltpu.VMEM((2, 2, 2, rows), jnp.int32),
            pltpu.VMEM((2, 3, prompts, width), f32),
            pltpu.VMEM((2, groups, width), bf16),
            pltpu.VMEM((2, width, hidden_slice), bf16),
            pltpu.VMEM((2, hidden_slice, width), bf16),
            pltpu.VMEM((4, groups, PAD, block_lanes), bf16),
            pltpu.VMEM((4, groups, PAD, block_lanes), bf16),
            pltpu.VMEM((4, 2, half, group_rows, width), bf16),
            pltpu.VMEM((4, 2, half, group_rows, width), bf16),
            pltpu.VMEM((4, half, group_rows, Z_FIRST), bf16),
            pltpu.VMEM((4, half, group_rows, Z_FIRST), bf16),
            pltpu.VMEM((4, half, group_rows, Z_FIRST), bf16),
            pltpu.VMEM((4, half, 2, group_rows, width - Z_FIRST), bf16),
            pltpu.VMEM((4, group_rows, width - Z_FIRST), bf16),
            pltpu.VMEM((4, group_rows, width - Z_FIRST), bf16),
            pltpu.VMEM((4, groups, PAD, block_lanes), bf16),
            pltpu.VMEM((4, groups, PAD, block_lanes), bf16),
            pltpu.VMEM((patch, 4 * rows), f32),
            pltpu.VMEM((SAMPLES, patch, 4 * rows), f32),
            pltpu.VMEM((keys, patch, 4 * rows), f32),
            pltpu.SemaphoreType.DMA((8, 4)),
            pltpu.SemaphoreType.DMA((14, 4)),
            pltpu.SemaphoreType.DMA((5,)),
            pltpu.SemaphoreType.DMA((5,)),
            pltpu.SemaphoreType.DMA((5,)),
            pltpu.SemaphoreType.DMA((4,)),
        ],
        compiler_params=pltpu.CompilerParams(
            has_side_effects=True, collective_id=0, vmem_limit_bytes=58 * 1024 * 1024
        ),
        name="flow_step",
    )(
        latents.transpose(0, 2, 1),
        cond,
        w_embed,
        modulation[0].transpose(1, 0, 2),
        router[0].T,
        w_in,
        w_out,
        routes[0].transpose(0, 2, 1),
        w_final.T,
    )
    next_rows, mean_map, var_map = pl.pallas_call(
        functools.partial(write_out, (members, groups // SAMPLES, rows)),
        out_shape=(
            jax.ShapeDtypeStruct((2, patch, rows), f32),
            jax.ShapeDtypeStruct((prompts, patch, members * rows), f32),
            jax.ShapeDtypeStruct((prompts, patch, members * rows), f32),
        ),
        in_specs=[vmem, vmem],
        out_specs=(vmem, vmem, vmem),
        name="write_out",
    )(maps, next_rows)
    return (next_rows.transpose(0, 2, 1), mean_map.transpose(0, 2, 1), var_map.transpose(0, 2, 1))


def solution(mesh):
    placed = (
        P(None, "expert", None),
        P(),
        P(),
        P("segment", None, None, None),
        P("segment", None, None),
        P("segment", "expert", None, None),
        P("segment", "expert", None, None),
        P("segment", None, "expert", None),
        P(),
    )
    return jax.shard_map(
        local,
        mesh=mesh,
        in_specs=placed,
        out_specs=(P("segment", "expert", None), P(), P()),
        check_vma=False,
    )
```

```python
import functools

import jax
import jax.numpy as jnp
from jax import lax
from jax.experimental import pallas as pl
from jax.experimental.pallas import tpu as pltpu
from jax.sharding import PartitionSpec as P

SAMPLES = 8
SEQ = 256
CAP = 5
PAD = 8
Z_FIRST = 768
ALONG_Y = 1024
PAIRS = 4

epsilon = 1e-06
time_step = 0.25
time_left = 0.5

f32 = jnp.float32
bf16 = jnp.bfloat16
MESH = pl.DeviceIdType.MESH


def normalize(values_in):
    centered = values_in - jnp.mean(values_in, axis=-1, keepdims=True)
    variance = jnp.mean(centered * centered, axis=-1, keepdims=True)
    return centered * lax.rsqrt(variance + epsilon)


def dot(left, right, over_left=1, over_right=0, **kwargs):
    dims = (((over_left,), (over_right,)), ((), ()))
    return lax.dot_general(left, right, dims, preferred_element_type=f32, **kwargs)


def iota(shape, dim):
    return lax.broadcasted_iota(jnp.int32, shape, dim)


def kernel(
    sizes,
    latents, cond, w_embed, modulation, router_in, w_first, w_second, routes_in, w_final,
    next_out, maps_out,
    hid, mix, routes, mods, router, first, second,
    out_send, out_recv, rows_in, rows_out, pair_recv, pair_send, own_recv, line_recv, line_send, cross_recv,
    home_send, home_recv, stats, stats_recv, maps,
    send_sems, recv_sems, load_sems, push_sems, land_sems, map_sems,
):
    groups, members, samples, rows, width, cut, along = sizes
    half = members // 2
    group_rows = groups * CAP
    slots = groups * PAD
    halves = groups // samples
    keys = 2 * halves * members
    core = lax.axis_index("segment")
    device = lax.axis_index("expert")
    group, member = device // members, device % members
    prompt_half, sample = group // samples, group % samples
    plane, place = member // half, member % half
    far_plane = 1 - plane
    other = 1 - core
    key = (core * halves + prompt_half) * members + member

    def expert_at(to_group, to_member):
        return {"expert": to_group * members + to_member}

    def in_group(to_plane, to_place):
        return expert_at(group, to_plane * half + to_place)

    def key_device(to_key):
        to_core = to_key // (halves * members)
        to_half = (to_key // members) % halves
        return {"segment": to_core, "expert": (to_half * samples + sample) * members + to_key % members}

    left, right = (place + half - 1) % half, (place + 1) % half

    row_x, pair = group // PAIRS, group % PAIRS
    own_slot = row_x * PAIRS

    def entry(to_group):
        away = (to_group % PAIRS - pair + PAIRS) % PAIRS
        odd, far = away % 2, away // 2
        to_plane = (far + (1 - odd) * plane) % 2
        slot = own_slot + odd * (1 + plane) + (1 - odd) * far * 3
        return expert_at(to_group, to_plane * half + place), slot

    def origin(slot):
        i = slot % PAIRS
        near, far = ((i + 1) // 2) % 2, i // 3
        from_pair = (pair + near * (2 * plane - 1) + far * 2 + PAIRS) % PAIRS
        from_plane = near * (i - 1) + (1 - near) * ((plane + far) % 2)
        return expert_at((slot // PAIRS) * PAIRS + from_pair, from_plane * half + place)

    barrier = pltpu.get_barrier_semaphore()

    def arrive(to):
        pl.semaphore_signal(barrier, inc=1, device_id=to, device_id_type=MESH)

    @pl.loop(1, groups)
    def _(k):
        arrive(entry((group + k) % groups)[0])
        arrive(origin((own_slot + k) % groups))

    @pl.loop(1, samples)
    def _(k):
        arrive(expert_at(prompt_half * samples + (sample + k) % samples, member))

    @pl.loop(1, members)
    def _(k):
        pl.semaphore_signal(
            barrier, inc=1, device_id=expert_at(group, (member + k) % members), device_id_type=MESH
        )

    @pl.loop(1, keys)
    def _(k):
        pl.semaphore_signal(barrier, inc=1, device_id=key_device((key + k) % keys), device_id_type=MESH)

    def load_pairs(micro_core):
        return [
            (routes_in.at[pl.ds(2 * micro_core, 2)], routes.at[core]),
            (router_in, router.at[core]),
            (modulation, mods.at[core]),
            (w_first.at[0, 0], first.at[core]),
            (w_second.at[0, 0], second.at[core]),
        ]

    own_loads = [
        pltpu.make_async_copy(src, dst, load_sems.at[i]) for i, (src, dst) in enumerate(load_pairs(core))
    ]
    pushes = [
        pltpu.make_async_remote_copy(
            src_ref=src, dst_ref=dst, send_sem=push_sems.at[i], recv_sem=land_sems.at[i],
            device_id={"segment": other}, device_id_type=MESH,
        )
        for i, (src, dst) in enumerate(load_pairs(other))
    ]
    for copy in own_loads:
        copy.start()

    frequency = jnp.exp(
        -jnp.log(jnp.full((1, width // 2), 10000.0, f32))
        * iota((1, width // 2), 1).astype(f32) / (width // 2)
    )
    position = (member * rows + iota((rows, 1), 0)).astype(f32)
    angles = position * frequency
    table = jnp.concatenate([jnp.sin(angles), jnp.cos(angles)], axis=1)
    for micro in range(2):
        prompt = (2 * core + micro) * halves + prompt_half
        embedded = dot(latents[2 * core + micro].T, w_embed[...], precision=lax.Precision.HIGHEST)
        hid[micro] = (embedded + table + cond[pl.ds(prompt, 1)]).astype(bf16)

    seg = width // 6
    half_width = width // 2

    def packing(shape, row_dim, part):
        row, slot = iota(shape, row_dim), iota(shape, 1 - row_dim)
        within, start = slot & (PAD - 1), CAP * (slot >> 3)
        if part < 2:
            hit = (row == start + (within & 3)) & ((within >> 2) == part)
        else:
            hit = (row == start + 4) & (within == part - 2)
        return jnp.where(hit, 1.0, 0.0).astype(bf16)

    def unpack_rows(low, last, matrix):
        parts = []
        for h in range(2):
            tail = jnp.concatenate([dot(matrix(2 + 3 * h + i), last) for i in range(3)], axis=1)
            parts.append(dot(matrix(h), low) + tail)
        return parts

    def pack_rows(full, matrix):
        low = dot(matrix(0), full[:, :half_width]) + dot(matrix(1), full[:, half_width:])
        last = dot(matrix(2), full[:, :seg])
        for i in range(1, 6):
            last = last + dot(matrix(2 + i), full[:, i * seg : (i + 1) * seg])
        return jnp.concatenate([low, last], axis=1).reshape(groups, PAD, 4 * seg).astype(bf16)

    def blocks_of(ref, unit):
        arrived = ref[unit].astype(f32).reshape(slots, 4 * seg).astype(bf16)
        return arrived[:, :half_width], arrived[:, half_width:]

    def wait_bytes(ref, sem):
        pltpu.make_async_copy(ref, ref, sem).wait()

    def send(source, target, send_sem, recv_sem, to):
        pltpu.make_async_remote_copy(
            src_ref=source, dst_ref=target, send_sem=send_sem, recv_sem=recv_sem,
            device_id=to, device_id_type=MESH,
        ).start()

    def send_out(unit):
        out_recv[unit, own_slot] = out_send[unit, group]

        @pl.loop(1, groups)
        def _(k):
            to_group = (group + k) % groups
            to, slot = entry(to_group)
            send(
                out_send.at[unit, to_group], out_recv.at[unit, slot],
                send_sems.at[0, unit], recv_sems.at[0, unit], to,
            )

    def send_back(unit):
        home_recv[unit, group] = home_send[unit, own_slot]

        @pl.loop(1, groups)
        def _(k):
            slot = (own_slot + k) % groups
            send(
                home_send.at[unit, slot], home_recv.at[unit, group],
                send_sems.at[6, unit], recv_sems.at[12, unit], origin(slot),
            )

    def front(layer, micro):
        unit = 2 * layer + micro
        prompt = (2 * core + micro) * halves + prompt_half
        shift, scale = mods[layer, 0, pl.ds(prompt, 1)], mods[layer, 1, pl.ds(prompt, 1)]
        normed = (normalize(hid[micro].astype(f32)) * (1.0 + scale) + shift).astype(bf16)
        logits = dot(router[layer], normed, 1, 1)
        chosen = routes[layer, micro]
        expert = iota((groups, rows), 0)
        slot = iota((slots, rows), 0)
        probs, hots = [], []
        for k in range(2):
            picked = jnp.sum(jnp.where(expert == chosen[k : k + 1], logits, 0.0), axis=0, keepdims=True)
            probs.append(lax.logistic(picked))
            hots.append((slot >> 3) == chosen[k : k + 1])
        both = jnp.where(hots[0] | hots[1], 1.0, 0.0)
        earlier = jnp.where(iota((rows, rows), 0) < iota((rows, rows), 1), 1.0, 0.0).astype(bf16)
        before = dot(both.astype(bf16), earlier)
        within = slot & (PAD - 1)
        mix[micro, 0] = (
            jnp.where(hots[0], probs[0], 0.0) + jnp.where(hots[1], probs[1], 0.0)
        ) / (probs[0] + probs[1])
        mix[micro, 1] = before

        def spread(part):
            if part < 2:
                hit = (before == (within & 3).astype(f32)) & ((within >> 2) == part)
            else:
                hit = (before == 4.0) & (within == part - 2)
            return jnp.where(hit, both, 0.0).astype(bf16)

        out_send[unit] = pack_rows(normed, spread)
        send_out(unit)

    def gather(layer, micro):
        unit = 2 * layer + micro
        wait_bytes(out_recv.at[unit, pl.ds(0, groups - 1)], recv_sems.at[0, unit])
        parts = unpack_rows(*blocks_of(out_recv, unit), lambda part: packing((group_rows, slots), 0, part))
        for h in range(2):
            rows_in[unit, plane, place, :, pl.ds(h * half_width, half_width)] = parts[h].astype(bf16)
        block = rows_in.at[unit, plane, place]
        send(block, block, send_sems.at[1, unit], recv_sems.at[1, unit], in_group(far_plane, place))
        send(block, block, send_sems.at[1, unit], recv_sems.at[2, unit], in_group(plane, right))
        send(block, block, send_sems.at[1, unit], recv_sems.at[3, unit], in_group(plane, left))

    def relay_across(layer, micro):
        unit = 2 * layer + micro
        wait_bytes(rows_in.at[unit, far_plane, place], recv_sems.at[1, unit])
        block = rows_in.at[unit, far_plane, place, :, pl.ds(0, along)]
        send(block, block, send_sems.at[7, unit], recv_sems.at[4, unit], in_group(plane, right))
        send(block, block, send_sems.at[7, unit], recv_sems.at[5, unit], in_group(plane, left))

    def cross(unit, from_place):
        block = rows_in.at[unit, plane, from_place, :, pl.ds(along, width - along)]
        send(block, block, send_sems.at[7, unit], recv_sems.at[13, unit], in_group(far_plane, place))

    def relay_own(layer, micro):
        unit = 2 * layer + micro
        wait_bytes(rows_in.at[unit, plane, left], recv_sems.at[2, unit])
        low = rows_in.at[unit, plane, left, :, pl.ds(0, half_width)]
        send(low, low, send_sems.at[7, unit], recv_sems.at[6, unit], in_group(plane, right))
        cross(unit, left)
        wait_bytes(rows_in.at[unit, plane, right], recv_sems.at[3, unit])
        high = rows_in.at[unit, plane, right, :, pl.ds(half_width, half_width)]
        send(high, high, send_sems.at[7, unit], recv_sems.at[6, unit], in_group(plane, left))
        cross(unit, right)

    def relay_far(layer, micro):
        unit = 2 * layer + micro
        wait_bytes(rows_in.at[unit, far_plane, left, :, pl.ds(0, along)], recv_sems.at[4, unit])
        low = rows_in.at[unit, far_plane, left, :, pl.ds(0, along // 2)]
        send(low, low, send_sems.at[7, unit], recv_sems.at[8, unit], in_group(plane, right))
        wait_bytes(rows_in.at[unit, far_plane, right, :, pl.ds(0, along)], recv_sems.at[5, unit])
        high = rows_in.at[unit, far_plane, right, :, pl.ds(along // 2, along // 2)]
        send(high, high, send_sems.at[7, unit], recv_sems.at[8, unit], in_group(plane, left))

    def relay_opposite(layer, micro):
        unit = 2 * layer + micro
        wait_bytes(rows_in.at[unit, plane, 0], recv_sems.at[6, unit])
        cross(unit, (place + 2) % half)

    def expert(unit, layer, of_plane):
        inner = dot(rows_in[unit, of_plane].reshape(half * group_rows, width), first[layer])
        inner = jax.nn.gelu(inner, approximate=True).astype(bf16)
        partial = dot(inner, second[layer]).astype(bf16)
        rows_out[unit, of_plane] = partial.reshape(half, group_rows, width)

        @pl.loop(1, half)
        def _(k):
            to_place = (place + k) % half
            send(
                rows_out.at[unit, of_plane, to_place, :, pl.ds(cut, width - cut)],
                line_recv.at[unit, place, of_plane],
                send_sems.at[3, unit], recv_sems.at[9, unit], in_group(plane, to_place),
            )

    def compute(layer, micro):
        unit = 2 * layer + micro

        @pl.loop(0, 2)
        def _(step):
            @pl.when(step == 1)
            def _():
                wait_bytes(rows_in.at[unit, far_plane, 0, :, pl.ds(0, along)], recv_sems.at[8, unit])
                wait_bytes(
                    rows_in.at[unit, far_plane, pl.ds(0, half - 1), :, pl.ds(along, width - along)],
                    recv_sems.at[13, unit],
                )

            expert(unit, layer, (plane + step) % 2)

        send(
            rows_out.at[unit, far_plane, :, :, pl.ds(0, cut)], pair_recv.at[unit],
            send_sems.at[2, unit], recv_sems.at[7, unit], in_group(far_plane, place),
        )
        for of_plane in range(2):
            line_recv[unit, place, of_plane] = rows_out[unit, of_plane, place, :, pl.ds(cut, width - cut)]

    def reduce_pair(layer, micro):
        unit = 2 * layer + micro
        wait_bytes(pair_recv.at[unit], recv_sems.at[7, unit])

        @pl.loop(0, half)
        def _(k):
            to_place = (place + 1 + k) % half
            mine = rows_out[unit, plane, to_place, :, pl.ds(0, cut)].astype(f32)
            pair_send[unit, to_place] = (mine + pair_recv[unit, to_place].astype(f32)).astype(bf16)

            @pl.when(k < half - 1)
            def _():
                send(
                    pair_send.at[unit, to_place], own_recv.at[unit, place],
                    send_sems.at[4, unit], recv_sems.at[10, unit], in_group(plane, to_place),
                )

        own_recv[unit, place] = pair_send[unit, place]

    def line_total(unit, of_plane):
        total = line_recv[unit, 0, of_plane].astype(f32)
        for k in range(1, half):
            total = total + line_recv[unit, k, of_plane].astype(f32)
        return total

    def reduce_line(layer, micro):
        unit = 2 * layer + micro
        wait_bytes(line_recv.at[unit, pl.ds(0, half - 1)], recv_sems.at[9, unit])
        line_send[unit] = line_total(unit, far_plane).astype(bf16)
        send(
            line_send.at[unit], cross_recv.at[unit],
            send_sems.at[5, unit], recv_sems.at[11, unit], in_group(far_plane, place),
        )

    def send_home(layer, micro):
        unit = 2 * layer + micro
        wait_bytes(own_recv.at[unit, pl.ds(0, half - 1)], recv_sems.at[10, unit])
        total = own_recv[unit, 0].astype(f32)
        for k in range(1, half):
            total = total + own_recv[unit, k].astype(f32)
        line = line_total(unit, plane)
        wait_bytes(cross_recv.at[unit], recv_sems.at[11, unit])
        line = line + cross_recv[unit].astype(f32)
        full = jnp.concatenate([total.astype(bf16), line.astype(bf16)], axis=1)
        home_send[unit] = pack_rows(full, lambda part: packing((slots, group_rows), 1, part))
        send_back(unit)

    def combine(layer, micro):
        unit = 2 * layer + micro
        wait_bytes(home_recv.at[unit, pl.ds(0, groups - 1)], recv_sems.at[12, unit])
        weights, before = mix[micro, 0].T, mix[micro, 1].T
        within = iota((rows, slots), 1) & (PAD - 1)

        def weighing(part):
            if part < 2:
                hit = (before == (within & 3).astype(f32)) & ((within >> 2) == part)
            else:
                hit = (before == 4.0) & (within == part - 2)
            kept = jnp.where(hit, weights, 0.0)
            coarse = kept.astype(bf16).astype(f32)
            return jnp.concatenate([coarse, kept - coarse], axis=0).astype(bf16)

        both = jnp.concatenate(unpack_rows(*blocks_of(home_recv, unit), weighing), axis=1)
        moe = both[:rows] + both[rows:]
        prompt = (2 * core + micro) * halves + prompt_half
        gate = mods[layer, 2, pl.ds(prompt, 1)]
        hid[micro] = (hid[micro].astype(f32) + gate * moe).astype(bf16)

    pl.semaphore_wait(barrier, 2 * (groups - 1) + samples - 1 + members - 1 + keys - 1)
    for copy in pushes:
        copy.start()

    for copy in own_loads[:3]:
        copy.wait()
    for copy in pushes[:3]:
        copy.wait_recv()

    for micro in range(2):
        front(0, micro)

    @pl.loop(0, 2)
    def _(layer):
        @pl.loop(0, 2)
        def _(micro):
            gather(layer, micro)

        @pl.loop(0, 2)
        def _(micro):
            relay_across(layer, micro)

        @pl.loop(0, 2)
        def _(micro):
            relay_own(layer, micro)

        @pl.loop(0, 2)
        def _(micro):
            relay_far(layer, micro)

        @pl.loop(0, 2)
        def _(micro):
            relay_opposite(layer, micro)

        @pl.when(layer == 0)
        def _():
            for copy in own_loads[3:]:
                copy.wait()
            for copy in pushes[3:]:
                copy.wait_recv()

        @pl.loop(0, 2)
        def _(micro):
            compute(layer, micro)

        @pl.loop(0, 2)
        def _(micro):
            reduce_pair(layer, micro)
            reduce_line(layer, micro)

        @pl.loop(0, 2)
        def _(micro):
            send_home(layer, micro)

        @pl.loop(0, 2)
        def _(micro):
            combine(layer, micro)

            @pl.when(layer == 0)
            def _():
                front(1, micro)

    pieces = []
    for micro in range(2):
        final = normalize(hid[micro].astype(f32)).astype(bf16)
        velocity = dot(w_final[...], final, 1, 1)
        start = latents[2 * core + micro]
        next_out[micro] = start + time_step * velocity
        clean = start + time_left * velocity
        pieces += [clean, clean * clean]
    stats[...] = jnp.concatenate(pieces, axis=1)
    stats_recv[sample] = stats[...]

    @pl.loop(1, samples)
    def _(k):
        to_sample = (sample + k) % samples
        send(
            stats, stats_recv.at[sample], map_sems.at[0], map_sems.at[1],
            expert_at(prompt_half * samples + to_sample, member),
        )

    wait_bytes(stats_recv.at[pl.ds(0, samples - 1)], map_sems.at[1])
    total = stats_recv[0]
    for k in range(1, samples):
        total = total + stats_recv[k]
    maps[key] = total

    @pl.loop(1, keys)
    def _(k):
        send(maps.at[key], maps.at[key], map_sems.at[2], map_sems.at[3], key_device((key + k) % keys))

    wait_bytes(maps.at[pl.ds(0, keys - 1)], map_sems.at[3])
    maps_out[...] = maps[...]

    for copy in pushes:
        copy.wait_send()
    wait_bytes(stats_recv.at[pl.ds(0, samples - 1)], map_sems.at[0])
    wait_bytes(maps.at[pl.ds(0, keys - 1)], map_sems.at[2])

    @pl.loop(0, 4)
    def _(unit):
        wait_bytes(out_recv.at[unit, pl.ds(0, groups - 1)], send_sems.at[0, unit])
        wait_bytes(out_recv.at[unit, pl.ds(0, groups - 1)], send_sems.at[6, unit])
        wait_bytes(rows_in.at[unit, 0], send_sems.at[7, unit])
        wait_bytes(rows_in.at[unit, 0, pl.ds(0, half - 1)], send_sems.at[1, unit])
        wait_bytes(pair_recv.at[unit], send_sems.at[2, unit])
        wait_bytes(line_recv.at[unit, pl.ds(0, half - 1)], send_sems.at[3, unit])
        wait_bytes(own_recv.at[unit, pl.ds(0, half - 1)], send_sems.at[4, unit])
        wait_bytes(line_send.at[unit], send_sems.at[5, unit])


def write_out(sizes, maps, next_in, next_out, mean_out, var_out):
    members, halves, rows = sizes
    next_out[...] = next_in[...]
    for core in range(2):
        for half in range(halves):
            blocks = [maps[(core * halves + half) * members + k] for k in range(members)]
            for micro in range(2):
                prompt = (2 * core + micro) * halves + half
                lanes = [slice((2 * micro + i) * rows, (2 * micro + i + 1) * rows) for i in range(2)]
                mean = jnp.concatenate([block[:, lanes[0]] for block in blocks], axis=1) / SAMPLES
                square = jnp.concatenate([block[:, lanes[1]] for block in blocks], axis=1) / SAMPLES
                mean_out[prompt] = mean
                var_out[prompt] = square - mean * mean


def local(latents, cond, w_embed, modulation, router, w_in, w_out, routes, w_final):
    devices = lax.axis_size("expert")
    rows, patch = latents.shape[1], latents.shape[2]
    width, groups = router.shape[1], router.shape[2]
    hidden_slice = w_in.shape[3]
    members = devices // groups
    half = members // 2
    slots = groups * PAD
    group_rows = groups * CAP
    prompts = cond.shape[0]
    keys = 2 * (groups // SAMPLES) * members

    vmem = pl.BlockSpec(memory_space=pltpu.VMEM)
    left = pl.BlockSpec(memory_space=pl.ANY)
    block_lanes = 4 * (width // 6)
    sizes = (groups, members, SAMPLES, rows, width, Z_FIRST, ALONG_Y)
    next_rows, maps = pl.pallas_call(
        functools.partial(kernel, sizes),
        out_shape=(
            jax.ShapeDtypeStruct((2, patch, rows), f32),
            jax.ShapeDtypeStruct((keys, patch, 4 * rows), f32),
        ),
        in_specs=[vmem, vmem, vmem, left, left, left, left, vmem, vmem],
        out_specs=(vmem, vmem),
        scratch_shapes=[
            pltpu.VMEM((2, rows, width), bf16),
            pltpu.VMEM((2, 2, slots, rows), f32),
            pltpu.VMEM((2, 2, 2, rows), jnp.int32),
            pltpu.VMEM((2, 3, prompts, width), f32),
            pltpu.VMEM((2, groups, width), bf16),
            pltpu.VMEM((2, width, hidden_slice), bf16),
            pltpu.VMEM((2, hidden_slice, width), bf16),
            pltpu.VMEM((4, groups, PAD, block_lanes), bf16),
            pltpu.VMEM((4, groups, PAD, block_lanes), bf16),
            pltpu.VMEM((4, 2, half, group_rows, width), bf16),
            pltpu.VMEM((4, 2, half, group_rows, width), bf16),
            pltpu.VMEM((4, half, group_rows, Z_FIRST), bf16),
            pltpu.VMEM((4, half, group_rows, Z_FIRST), bf16),
            pltpu.VMEM((4, half, group_rows, Z_FIRST), bf16),
            pltpu.VMEM((4, half, 2, group_rows, width - Z_FIRST), bf16),
            pltpu.VMEM((4, group_rows, width - Z_FIRST), bf16),
            pltpu.VMEM((4, group_rows, width - Z_FIRST), bf16),
            pltpu.VMEM((4, groups, PAD, block_lanes), bf16),
            pltpu.VMEM((4, groups, PAD, block_lanes), bf16),
            pltpu.VMEM((patch, 4 * rows), f32),
            pltpu.VMEM((SAMPLES, patch, 4 * rows), f32),
            pltpu.VMEM((keys, patch, 4 * rows), f32),
            pltpu.SemaphoreType.DMA((8, 4)),
            pltpu.SemaphoreType.DMA((14, 4)),
            pltpu.SemaphoreType.DMA((5,)),
            pltpu.SemaphoreType.DMA((5,)),
            pltpu.SemaphoreType.DMA((5,)),
            pltpu.SemaphoreType.DMA((4,)),
        ],
        compiler_params=pltpu.CompilerParams(
            has_side_effects=True, collective_id=0, vmem_limit_bytes=58 * 1024 * 1024
        ),
        name="flow_step",
    )(
        latents.transpose(0, 2, 1),
        cond,
        w_embed,
        modulation[0].transpose(1, 0, 2),
        router[0].T,
        w_in,
        w_out,
        routes[0].transpose(0, 2, 1),
        w_final.T,
    )
    next_rows, mean_map, var_map = pl.pallas_call(
        functools.partial(write_out, (members, groups // SAMPLES, rows)),
        out_shape=(
            jax.ShapeDtypeStruct((2, patch, rows), f32),
            jax.ShapeDtypeStruct((prompts, patch, members * rows), f32),
            jax.ShapeDtypeStruct((prompts, patch, members * rows), f32),
        ),
        in_specs=[vmem, vmem],
        out_specs=(vmem, vmem, vmem),
        name="write_out",
    )(maps, next_rows)
    return (next_rows.transpose(0, 2, 1), mean_map.transpose(0, 2, 1), var_map.transpose(0, 2, 1))


def solution(mesh):
    placed = (
        P(None, "expert", None),
        P(),
        P(),
        P("segment", None, None, None),
        P("segment", None, None),
        P("segment", "expert", None, None),
        P("segment", "expert", None, None),
        P("segment", None, "expert", None),
        P(),
    )
    return jax.shard_map(
        local,
        mesh=mesh,
        in_specs=placed,
        out_specs=(P("segment", "expert", None), P(), P()),
        check_vma=False,
    )
```

```python
import functools

import jax
import jax.numpy as jnp
from jax import lax
from jax.experimental import pallas as pl
from jax.experimental.pallas import tpu as pltpu
from jax.sharding import PartitionSpec as P

SAMPLES = 8
SEQ = 256
CAP = 5
PAD = 8
Z_FIRST = 512
ALONG_Y = 1024
PAIRS = 4

epsilon = 1e-06
time_step = 0.25
time_left = 0.5

f32 = jnp.float32
bf16 = jnp.bfloat16
MESH = pl.DeviceIdType.MESH


def normalize(values_in):
    centered = values_in - jnp.mean(values_in, axis=-1, keepdims=True)
    variance = jnp.mean(centered * centered, axis=-1, keepdims=True)
    return centered * lax.rsqrt(variance + epsilon)


def dot(left, right, over_left=1, over_right=0, **kwargs):
    dims = (((over_left,), (over_right,)), ((), ()))
    return lax.dot_general(left, right, dims, preferred_element_type=f32, **kwargs)


def iota(shape, dim):
    return lax.broadcasted_iota(jnp.int32, shape, dim)


def kernel(
    sizes,
    latents, cond, w_embed, modulation, router_in, w_first, w_second, routes_in, w_final,
    next_out, maps_out,
    hid, mix, routes, mods, router, first, second,
    out_send, out_recv, rows_in, rows_out, pair_recv, pairs, pair_step, pair_turn, line_step, line_turn, line_send,
    cross_recv,
    home_send, home_recv, stats, stats_recv, maps,
    send_sems, recv_sems, load_sems, push_sems, land_sems, map_sems,
):
    groups, members, samples, rows, width, cut, along = sizes
    half = members // 2
    group_rows = groups * CAP
    slots = groups * PAD
    halves = groups // samples
    keys = 2 * halves * members
    core = lax.axis_index("segment")
    device = lax.axis_index("expert")
    group, member = device // members, device % members
    prompt_half, sample = group // samples, group % samples
    plane, place = member // half, member % half
    far_plane = 1 - plane
    other = 1 - core
    key = (core * halves + prompt_half) * members + member

    def expert_at(to_group, to_member):
        return {"expert": to_group * members + to_member}

    def in_group(to_plane, to_place):
        return expert_at(group, to_plane * half + to_place)

    def key_device(to_key):
        to_core = to_key // (halves * members)
        to_half = (to_key // members) % halves
        return {"segment": to_core, "expert": (to_half * samples + sample) * members + to_key % members}

    left, right, opposite = (place + half - 1) % half, (place + 1) % half, (place + 2) % half

    def pair_half(side):
        return pl.ds(side * (cut // 2), cut // 2)

    def line_half(side):
        return pl.ds(cut + side * ((width - cut) // 2), (width - cut) // 2)

    row_x, pair = group // PAIRS, group % PAIRS
    own_slot = row_x * PAIRS

    def entry(to_group):
        away = (to_group % PAIRS - pair + PAIRS) % PAIRS
        odd, far = away % 2, away // 2
        to_plane = (far + (1 - odd) * plane) % 2
        slot = own_slot + odd * (1 + plane) + (1 - odd) * far * 3
        return expert_at(to_group, to_plane * half + place), slot

    def origin(slot):
        i = slot % PAIRS
        near, far = ((i + 1) // 2) % 2, i // 3
        from_pair = (pair + near * (2 * plane - 1) + far * 2 + PAIRS) % PAIRS
        from_plane = near * (i - 1) + (1 - near) * ((plane + far) % 2)
        return expert_at((slot // PAIRS) * PAIRS + from_pair, from_plane * half + place)

    barrier = pltpu.get_barrier_semaphore()

    def arrive(to):
        pl.semaphore_signal(barrier, inc=1, device_id=to, device_id_type=MESH)

    @pl.loop(1, groups)
    def _(k):
        arrive(entry((group + k) % groups)[0])
        arrive(origin((own_slot + k) % groups))

    @pl.loop(1, samples)
    def _(k):
        arrive(expert_at(prompt_half * samples + (sample + k) % samples, member))

    @pl.loop(1, members)
    def _(k):
        pl.semaphore_signal(
            barrier, inc=1, device_id=expert_at(group, (member + k) % members), device_id_type=MESH
        )

    @pl.loop(1, keys)
    def _(k):
        pl.semaphore_signal(barrier, inc=1, device_id=key_device((key + k) % keys), device_id_type=MESH)

    def load_pairs(micro_core):
        return [
            (routes_in.at[pl.ds(2 * micro_core, 2)], routes.at[core]),
            (router_in, router.at[core]),
            (modulation, mods.at[core]),
            (w_first.at[0, 0], first.at[core]),
            (w_second.at[0, 0], second.at[core]),
        ]

    own_loads = [
        pltpu.make_async_copy(src, dst, load_sems.at[i]) for i, (src, dst) in enumerate(load_pairs(core))
    ]
    pushes = [
        pltpu.make_async_remote_copy(
            src_ref=src, dst_ref=dst, send_sem=push_sems.at[i], recv_sem=land_sems.at[i],
            device_id={"segment": other}, device_id_type=MESH,
        )
        for i, (src, dst) in enumerate(load_pairs(other))
    ]
    for copy in own_loads:
        copy.start()

    frequency = jnp.exp(
        -jnp.log(jnp.full((1, width // 2), 10000.0, f32))
        * iota((1, width // 2), 1).astype(f32) / (width // 2)
    )
    position = (member * rows + iota((rows, 1), 0)).astype(f32)
    angles = position * frequency
    table = jnp.concatenate([jnp.sin(angles), jnp.cos(angles)], axis=1)
    for micro in range(2):
        prompt = (2 * core + micro) * halves + prompt_half
        embedded = dot(latents[2 * core + micro].T, w_embed[...], precision=lax.Precision.HIGHEST)
        hid[micro] = (embedded + table + cond[pl.ds(prompt, 1)]).astype(bf16)

    seg = width // 6
    half_width = width // 2

    def packing(shape, row_dim, part):
        row, slot = iota(shape, row_dim), iota(shape, 1 - row_dim)
        within, start = slot & (PAD - 1), CAP * (slot >> 3)
        if part < 2:
            hit = (row == start + (within & 3)) & ((within >> 2) == part)
        else:
            hit = (row == start + 4) & (within == part - 2)
        return jnp.where(hit, 1.0, 0.0).astype(bf16)

    def unpack_rows(low, last, matrix):
        parts = []
        for h in range(2):
            tail = jnp.concatenate([dot(matrix(2 + 3 * h + i), last) for i in range(3)], axis=1)
            parts.append(dot(matrix(h), low) + tail)
        return parts

    def pack_rows(full, matrix):
        low = dot(matrix(0), full[:, :half_width]) + dot(matrix(1), full[:, half_width:])
        last = dot(matrix(2), full[:, :seg])
        for i in range(1, 6):
            last = last + dot(matrix(2 + i), full[:, i * seg : (i + 1) * seg])
        return jnp.concatenate([low, last], axis=1).reshape(groups, PAD, 4 * seg).astype(bf16)

    def blocks_of(ref, unit):
        arrived = ref[unit].astype(f32).reshape(slots, 4 * seg).astype(bf16)
        return arrived[:, :half_width], arrived[:, half_width:]

    def wait_bytes(ref, sem):
        pltpu.make_async_copy(ref, ref, sem).wait()

    def send(source, target, send_sem, recv_sem, to):
        pltpu.make_async_remote_copy(
            src_ref=source, dst_ref=target, send_sem=send_sem, recv_sem=recv_sem,
            device_id=to, device_id_type=MESH,
        ).start()

    def send_out(unit):
        out_recv[unit, own_slot] = out_send[unit, group]

        @pl.loop(1, groups)
        def _(k):
            to_group = (group + k) % groups
            to, slot = entry(to_group)
            send(
                out_send.at[unit, to_group], out_recv.at[unit, slot],
                send_sems.at[0, unit], recv_sems.at[0, unit], to,
            )

    def send_back(unit):
        home_recv[unit, group] = home_send[unit, own_slot]

        @pl.loop(1, groups)
        def _(k):
            slot = (own_slot + k) % groups
            send(
                home_send.at[unit, slot], home_recv.at[unit, group],
                send_sems.at[6, unit], recv_sems.at[12, unit], origin(slot),
            )

    def front(layer, micro):
        unit = 2 * layer + micro
        prompt = (2 * core + micro) * halves + prompt_half
        shift, scale = mods[layer, 0, pl.ds(prompt, 1)], mods[layer, 1, pl.ds(prompt, 1)]
        normed = (normalize(hid[micro].astype(f32)) * (1.0 + scale) + shift).astype(bf16)
        logits = dot(router[layer], normed, 1, 1)
        chosen = routes[layer, micro]
        expert = iota((groups, rows), 0)
        slot = iota((slots, rows), 0)
        probs, hots = [], []
        for k in range(2):
            picked = jnp.sum(jnp.where(expert == chosen[k : k + 1], logits, 0.0), axis=0, keepdims=True)
            probs.append(lax.logistic(picked))
            hots.append((slot >> 3) == chosen[k : k + 1])
        both = jnp.where(hots[0] | hots[1], 1.0, 0.0)
        earlier = jnp.where(iota((rows, rows), 0) < iota((rows, rows), 1), 1.0, 0.0).astype(bf16)
        before = dot(both.astype(bf16), earlier)
        within = slot & (PAD - 1)
        mix[micro, 0] = (
            jnp.where(hots[0], probs[0], 0.0) + jnp.where(hots[1], probs[1], 0.0)
        ) / (probs[0] + probs[1])
        mix[micro, 1] = before

        def spread(part):
            if part < 2:
                hit = (before == (within & 3).astype(f32)) & ((within >> 2) == part)
            else:
                hit = (before == 4.0) & (within == part - 2)
            return jnp.where(hit, both, 0.0).astype(bf16)

        out_send[unit] = pack_rows(normed, spread)
        send_out(unit)

    def gather(layer, micro):
        unit = 2 * layer + micro
        wait_bytes(out_recv.at[unit, pl.ds(0, groups - 1)], recv_sems.at[0, unit])
        parts = unpack_rows(*blocks_of(out_recv, unit), lambda part: packing((group_rows, slots), 0, part))
        for h in range(2):
            rows_in[unit, plane, place, :, pl.ds(h * half_width, half_width)] = parts[h].astype(bf16)
        block = rows_in.at[unit, plane, place]
        send(block, block, send_sems.at[1, unit], recv_sems.at[1, unit], in_group(far_plane, place))
        send(block, block, send_sems.at[1, unit], recv_sems.at[2, unit], in_group(plane, right))
        send(block, block, send_sems.at[1, unit], recv_sems.at[3, unit], in_group(plane, left))

    def relay_across(layer, micro):
        unit = 2 * layer + micro
        wait_bytes(rows_in.at[unit, far_plane, place], recv_sems.at[1, unit])
        block = rows_in.at[unit, far_plane, place, :, pl.ds(0, along)]
        send(block, block, send_sems.at[7, unit], recv_sems.at[4, unit], in_group(plane, right))
        send(block, block, send_sems.at[7, unit], recv_sems.at[5, unit], in_group(plane, left))

    def cross(unit, from_place):
        block = rows_in.at[unit, plane, from_place, :, pl.ds(along, width - along)]
        send(block, block, send_sems.at[7, unit], recv_sems.at[13, unit], in_group(far_plane, place))

    def relay_own(layer, micro):
        unit = 2 * layer + micro
        wait_bytes(rows_in.at[unit, plane, left], recv_sems.at[2, unit])
        low = rows_in.at[unit, plane, left, :, pl.ds(0, half_width)]
        send(low, low, send_sems.at[7, unit], recv_sems.at[6, unit], in_group(plane, right))
        cross(unit, left)
        wait_bytes(rows_in.at[unit, plane, right], recv_sems.at[3, unit])
        high = rows_in.at[unit, plane, right, :, pl.ds(half_width, half_width)]
        send(high, high, send_sems.at[7, unit], recv_sems.at[6, unit], in_group(plane, left))
        cross(unit, right)

    def relay_far(layer, micro):
        unit = 2 * layer + micro
        wait_bytes(rows_in.at[unit, far_plane, left, :, pl.ds(0, along)], recv_sems.at[4, unit])
        low = rows_in.at[unit, far_plane, left, :, pl.ds(0, along // 2)]
        send(low, low, send_sems.at[7, unit], recv_sems.at[8, unit], in_group(plane, right))
        wait_bytes(rows_in.at[unit, far_plane, right, :, pl.ds(0, along)], recv_sems.at[5, unit])
        high = rows_in.at[unit, far_plane, right, :, pl.ds(along // 2, along // 2)]
        send(high, high, send_sems.at[7, unit], recv_sems.at[8, unit], in_group(plane, left))

    def relay_opposite(layer, micro):
        unit = 2 * layer + micro
        wait_bytes(rows_in.at[unit, plane, 0], recv_sems.at[6, unit])
        cross(unit, opposite)

    def expert(unit, layer, of_plane):
        inner = dot(rows_in[unit, of_plane].reshape(half * group_rows, width), first[layer])
        inner = jax.nn.gelu(inner, approximate=True).astype(bf16)
        partial = dot(inner, second[layer]).astype(bf16)
        rows_out[unit, of_plane] = partial.reshape(half, group_rows, width)

        for side in range(2):
            send(
                rows_out.at[unit, of_plane, opposite, :, line_half(side)], line_step.at[unit, side, of_plane],
                send_sems.at[3, unit], recv_sems.at[9, unit], in_group(plane, (right, left)[side]),
            )

    def compute(layer, micro):
        unit = 2 * layer + micro

        @pl.loop(0, 2)
        def _(step):
            @pl.when(step == 1)
            def _():
                wait_bytes(rows_in.at[unit, far_plane, 0, :, pl.ds(0, along)], recv_sems.at[8, unit])
                wait_bytes(
                    rows_in.at[unit, far_plane, pl.ds(0, half - 1), :, pl.ds(along, width - along)],
                    recv_sems.at[13, unit],
                )

            expert(unit, layer, (plane + step) % 2)

        send(
            rows_out.at[unit, far_plane, :, :, pl.ds(0, cut)], pair_recv.at[unit],
            send_sems.at[2, unit], recv_sems.at[7, unit], in_group(far_plane, place),
        )
    def turn_line(layer, micro):
        unit = 2 * layer + micro
        wait_bytes(line_step.at[unit], recv_sems.at[9, unit])
        for side, to_place in enumerate((right, left)):
            for of_plane in range(2):
                mine = rows_out[unit, of_plane, to_place, :, line_half(side)].astype(f32)
                rows_out[unit, of_plane, to_place, :, line_half(side)] = (
                    mine + line_step[unit, side, of_plane].astype(f32)
                ).astype(bf16)
            send(
                rows_out.at[unit, :, to_place, :, pl.ds(cut, width - cut)], line_turn.at[unit, side],
                send_sems.at[8, unit], recv_sems.at[14, unit], in_group(plane, to_place),
            )

    def reduce_pair(layer, micro):
        unit = 2 * layer + micro
        wait_bytes(pair_recv.at[unit], recv_sems.at[7, unit])
        pairs[unit] = (
            rows_out[unit, plane, :, :, pl.ds(0, cut)].astype(f32) + pair_recv[unit].astype(f32)
        ).astype(bf16)
        for side in range(2):
            send(
                pairs.at[unit, opposite, :, pair_half(side)], pair_step.at[unit, side],
                send_sems.at[4, unit], recv_sems.at[10, unit], in_group(plane, (right, left)[side]),
            )

    def turn_pair(layer, micro):
        unit = 2 * layer + micro
        wait_bytes(pair_step.at[unit], recv_sems.at[10, unit])
        for side, to_place in enumerate((right, left)):
            mine = pairs[unit, to_place, :, pair_half(side)].astype(f32)
            pairs[unit, to_place, :, pair_half(side)] = (mine + pair_step[unit, side].astype(f32)).astype(bf16)
            send(
                pairs.at[unit, to_place], pair_turn.at[unit, side],
                send_sems.at[9, unit], recv_sems.at[15, unit], in_group(plane, to_place),
            )

    def line_total(unit, of_plane):
        mine = rows_out[unit, of_plane, place, :, pl.ds(cut, width - cut)].astype(f32)
        return mine + line_turn[unit, 0, of_plane].astype(f32) + line_turn[unit, 1, of_plane].astype(f32)

    def reduce_line(layer, micro):
        unit = 2 * layer + micro
        wait_bytes(line_turn.at[unit], recv_sems.at[14, unit])
        line_send[unit] = line_total(unit, far_plane).astype(bf16)
        send(
            line_send.at[unit], cross_recv.at[unit],
            send_sems.at[5, unit], recv_sems.at[11, unit], in_group(far_plane, place),
        )

    def send_home(layer, micro):
        unit = 2 * layer + micro
        wait_bytes(pair_turn.at[unit], recv_sems.at[15, unit])
        total = pairs[unit, place].astype(f32)
        for side in range(2):
            total = total + pair_turn[unit, side].astype(f32)
        line = line_total(unit, plane)
        wait_bytes(cross_recv.at[unit], recv_sems.at[11, unit])
        line = line + cross_recv[unit].astype(f32)
        full = jnp.concatenate([total.astype(bf16), line.astype(bf16)], axis=1)
        home_send[unit] = pack_rows(full, lambda part: packing((slots, group_rows), 1, part))
        send_back(unit)

    def combine(layer, micro):
        unit = 2 * layer + micro
        wait_bytes(home_recv.at[unit, pl.ds(0, groups - 1)], recv_sems.at[12, unit])
        weights, before = mix[micro, 0].T, mix[micro, 1].T
        within = iota((rows, slots), 1) & (PAD - 1)

        def weighing(part):
            if part < 2:
                hit = (before == (within & 3).astype(f32)) & ((within >> 2) == part)
            else:
                hit = (before == 4.0) & (within == part - 2)
            kept = jnp.where(hit, weights, 0.0)
            coarse = kept.astype(bf16).astype(f32)
            return jnp.concatenate([coarse, kept - coarse], axis=0).astype(bf16)

        both = jnp.concatenate(unpack_rows(*blocks_of(home_recv, unit), weighing), axis=1)
        moe = both[:rows] + both[rows:]
        prompt = (2 * core + micro) * halves + prompt_half
        gate = mods[layer, 2, pl.ds(prompt, 1)]
        hid[micro] = (hid[micro].astype(f32) + gate * moe).astype(bf16)

    pl.semaphore_wait(barrier, 2 * (groups - 1) + samples - 1 + members - 1 + keys - 1)
    for copy in pushes:
        copy.start()

    for copy in own_loads[:3]:
        copy.wait()
    for copy in pushes[:3]:
        copy.wait_recv()

    for micro in range(2):
        front(0, micro)

    @pl.loop(0, 2)
    def _(layer):
        @pl.loop(0, 2)
        def _(micro):
            gather(layer, micro)

        @pl.loop(0, 2)
        def _(micro):
            relay_across(layer, micro)

        @pl.loop(0, 2)
        def _(micro):
            relay_own(layer, micro)

        @pl.loop(0, 2)
        def _(micro):
            relay_far(layer, micro)

        @pl.loop(0, 2)
        def _(micro):
            relay_opposite(layer, micro)

        @pl.when(layer == 0)
        def _():
            for copy in own_loads[3:]:
                copy.wait()
            for copy in pushes[3:]:
                copy.wait_recv()

        @pl.loop(0, 2)
        def _(micro):
            compute(layer, micro)

        @pl.loop(0, 2)
        def _(micro):
            turn_line(layer, micro)
            reduce_pair(layer, micro)

        @pl.loop(0, 2)
        def _(micro):
            turn_pair(layer, micro)
            reduce_line(layer, micro)

        @pl.loop(0, 2)
        def _(micro):
            send_home(layer, micro)

        @pl.loop(0, 2)
        def _(micro):
            combine(layer, micro)

            @pl.when(layer == 0)
            def _():
                front(1, micro)

    pieces = []
    for micro in range(2):
        final = normalize(hid[micro].astype(f32)).astype(bf16)
        velocity = dot(w_final[...], final, 1, 1)
        start = latents[2 * core + micro]
        next_out[micro] = start + time_step * velocity
        clean = start + time_left * velocity
        pieces += [clean, clean * clean]
    stats[...] = jnp.concatenate(pieces, axis=1)
    stats_recv[sample] = stats[...]

    @pl.loop(1, samples)
    def _(k):
        to_sample = (sample + k) % samples
        send(
            stats, stats_recv.at[sample], map_sems.at[0], map_sems.at[1],
            expert_at(prompt_half * samples + to_sample, member),
        )

    wait_bytes(stats_recv.at[pl.ds(0, samples - 1)], map_sems.at[1])
    total = stats_recv[0]
    for k in range(1, samples):
        total = total + stats_recv[k]
    maps[key] = total

    @pl.loop(1, keys)
    def _(k):
        send(maps.at[key], maps.at[key], map_sems.at[2], map_sems.at[3], key_device((key + k) % keys))

    wait_bytes(maps.at[pl.ds(0, keys - 1)], map_sems.at[3])
    maps_out[...] = maps[...]

    for copy in pushes:
        copy.wait_send()
    wait_bytes(stats_recv.at[pl.ds(0, samples - 1)], map_sems.at[0])
    wait_bytes(maps.at[pl.ds(0, keys - 1)], map_sems.at[2])

    @pl.loop(0, 4)
    def _(unit):
        wait_bytes(out_recv.at[unit, pl.ds(0, groups - 1)], send_sems.at[0, unit])
        wait_bytes(out_recv.at[unit, pl.ds(0, groups - 1)], send_sems.at[6, unit])
        wait_bytes(rows_in.at[unit, 0], send_sems.at[7, unit])
        wait_bytes(rows_in.at[unit, 0, pl.ds(0, half - 1)], send_sems.at[1, unit])
        wait_bytes(pair_recv.at[unit], send_sems.at[2, unit])
        wait_bytes(line_step.at[unit], send_sems.at[3, unit])
        wait_bytes(pair_step.at[unit], send_sems.at[4, unit])
        wait_bytes(line_turn.at[unit], send_sems.at[8, unit])
        wait_bytes(pair_turn.at[unit], send_sems.at[9, unit])
        wait_bytes(line_send.at[unit], send_sems.at[5, unit])


def write_out(sizes, maps, next_in, next_out, mean_out, var_out):
    members, halves, rows = sizes
    next_out[...] = next_in[...]
    for core in range(2):
        for half in range(halves):
            blocks = [maps[(core * halves + half) * members + k] for k in range(members)]
            for micro in range(2):
                prompt = (2 * core + micro) * halves + half
                lanes = [slice((2 * micro + i) * rows, (2 * micro + i + 1) * rows) for i in range(2)]
                mean = jnp.concatenate([block[:, lanes[0]] for block in blocks], axis=1) / SAMPLES
                square = jnp.concatenate([block[:, lanes[1]] for block in blocks], axis=1) / SAMPLES
                mean_out[prompt] = mean
                var_out[prompt] = square - mean * mean


def local(latents, cond, w_embed, modulation, router, w_in, w_out, routes, w_final):
    devices = lax.axis_size("expert")
    rows, patch = latents.shape[1], latents.shape[2]
    width, groups = router.shape[1], router.shape[2]
    hidden_slice = w_in.shape[3]
    members = devices // groups
    half = members // 2
    slots = groups * PAD
    group_rows = groups * CAP
    prompts = cond.shape[0]
    keys = 2 * (groups // SAMPLES) * members

    vmem = pl.BlockSpec(memory_space=pltpu.VMEM)
    left = pl.BlockSpec(memory_space=pl.ANY)
    block_lanes = 4 * (width // 6)
    sizes = (groups, members, SAMPLES, rows, width, Z_FIRST, ALONG_Y)
    next_rows, maps = pl.pallas_call(
        functools.partial(kernel, sizes),
        out_shape=(
            jax.ShapeDtypeStruct((2, patch, rows), f32),
            jax.ShapeDtypeStruct((keys, patch, 4 * rows), f32),
        ),
        in_specs=[vmem, vmem, vmem, left, left, left, left, vmem, vmem],
        out_specs=(vmem, vmem),
        scratch_shapes=[
            pltpu.VMEM((2, rows, width), bf16),
            pltpu.VMEM((2, 2, slots, rows), f32),
            pltpu.VMEM((2, 2, 2, rows), jnp.int32),
            pltpu.VMEM((2, 3, prompts, width), f32),
            pltpu.VMEM((2, groups, width), bf16),
            pltpu.VMEM((2, width, hidden_slice), bf16),
            pltpu.VMEM((2, hidden_slice, width), bf16),
            pltpu.VMEM((4, groups, PAD, block_lanes), bf16),
            pltpu.VMEM((4, groups, PAD, block_lanes), bf16),
            pltpu.VMEM((4, 2, half, group_rows, width), bf16),
            pltpu.VMEM((4, 2, half, group_rows, width), bf16),
            pltpu.VMEM((4, half, group_rows, Z_FIRST), bf16),
            pltpu.VMEM((4, half, group_rows, Z_FIRST), bf16),
            pltpu.VMEM((4, 2, group_rows, Z_FIRST // 2), bf16),
            pltpu.VMEM((4, 2, group_rows, Z_FIRST), bf16),
            pltpu.VMEM((4, 2, 2, group_rows, (width - Z_FIRST) // 2), bf16),
            pltpu.VMEM((4, 2, 2, group_rows, width - Z_FIRST), bf16),
            pltpu.VMEM((4, group_rows, width - Z_FIRST), bf16),
            pltpu.VMEM((4, group_rows, width - Z_FIRST), bf16),
            pltpu.VMEM((4, groups, PAD, block_lanes), bf16),
            pltpu.VMEM((4, groups, PAD, block_lanes), bf16),
            pltpu.VMEM((patch, 4 * rows), f32),
            pltpu.VMEM((SAMPLES, patch, 4 * rows), f32),
            pltpu.VMEM((keys, patch, 4 * rows), f32),
            pltpu.SemaphoreType.DMA((10, 4)),
            pltpu.SemaphoreType.DMA((16, 4)),
            pltpu.SemaphoreType.DMA((5,)),
            pltpu.SemaphoreType.DMA((5,)),
            pltpu.SemaphoreType.DMA((5,)),
            pltpu.SemaphoreType.DMA((4,)),
        ],
        compiler_params=pltpu.CompilerParams(
            has_side_effects=True, collective_id=0, vmem_limit_bytes=58 * 1024 * 1024
        ),
        name="flow_step",
    )(
        latents.transpose(0, 2, 1),
        cond,
        w_embed,
        modulation[0].transpose(1, 0, 2),
        router[0].T,
        w_in,
        w_out,
        routes[0].transpose(0, 2, 1),
        w_final.T,
    )
    next_rows, mean_map, var_map = pl.pallas_call(
        functools.partial(write_out, (members, groups // SAMPLES, rows)),
        out_shape=(
            jax.ShapeDtypeStruct((2, patch, rows), f32),
            jax.ShapeDtypeStruct((prompts, patch, members * rows), f32),
            jax.ShapeDtypeStruct((prompts, patch, members * rows), f32),
        ),
        in_specs=[vmem, vmem],
        out_specs=(vmem, vmem, vmem),
        name="write_out",
    )(maps, next_rows)
    return (next_rows.transpose(0, 2, 1), mean_map.transpose(0, 2, 1), var_map.transpose(0, 2, 1))


def solution(mesh):
    placed = (
        P(None, "expert", None),
        P(),
        P(),
        P("segment", None, None, None),
        P("segment", None, None),
        P("segment", "expert", None, None),
        P("segment", "expert", None, None),
        P("segment", None, "expert", None),
        P(),
    )
    return jax.shard_map(
        local,
        mesh=mesh,
        in_specs=placed,
        out_specs=(P("segment", "expert", None), P(), P()),
        check_vma=False,
    )
```
